32 devices in a mesh: ctx: 4 (over y, x), fsdp: 8 (over z, core).
Axes of the slice: x: 2, y: 2, z: 4, core: 2. Of those that a mesh axis runs over, the one named last changes fastest.
Arguments:
- hidden_in: bfloat16 [8, 1024, 1536], P('fsdp', 'ctx'), may hold values from -6 to 6
- norm_attn: bfloat16 [1536], P('fsdp'), may hold values from 0.5 to 1.5
- w_qkv: bfloat16 [1536, 2560], P('fsdp'), may hold values from -1 to 1
- w_mix: bfloat16 [1536, 1536], P('fsdp'), may hold values from -2.5 to 2.5
- norm_moe: bfloat16 [1536], P('fsdp'), may hold values from 0.5 to 1.5
- w_in: bfloat16 [16, 1536, 1024], P('fsdp'), may hold values from -0.15625 to 0.15625
- w_out: bfloat16 [16, 1536, 512], P('fsdp'), may hold values from -1 to 1
- routes: int32 [8, 1024, 8], P('fsdp', 'ctx'), may hold values from 0 to 15, all different within a row; in each aligned block of 256 rows (0 to 255, 256 to 511, ..., all dimensions but the last counted through in order) at most 160 rows name the same one
- gates: float32 [8, 1024, 8], P('fsdp', 'ctx'), may hold values from 0.05 to 0.5
- cotangent: bfloat16 [8, 1024, 1536], P('fsdp', 'ctx'), may hold values from -6 to 6
Outputs:
- hidden_out: bfloat16 [8, 1024, 1536], P('fsdp', 'ctx')
- grad_hidden: float32 [8, 1024, 1536], P('fsdp', 'ctx')
- grad_norm_attn: float32 [1536], P('fsdp')
- grad_w_qkv: float32 [1536, 2560], P('fsdp')
- grad_w_mix: float32 [1536, 1536], P('fsdp')
- grad_norm_moe: float32 [1536], P('fsdp')
- grad_w_in: float32 [16, 1536, 1024], P('fsdp', 'ctx')
- grad_w_out: float32 [16, 1536, 512], P('fsdp', 'ctx')
- grad_gates: float32 [8, 1024, 8], P('fsdp', 'ctx')
The draws below stay inside these ranges and needn't reach their ends.
Inputs may be any that keep to these rules, and one draw needn't show every extreme that they name: `routes`: in each aligned block of 256 positions of a sequence no expert is named by more than 160 rows, and in some block an expert is named by exactly 160; each row names 8 different experts.
All inputs are finite; a program needn't handle non-finite values.
Results may differ from the reference program's by a relative error of at most 0.024.
Values may be sent and summed in bfloat16 or wider, within the bound.
No kernel may reach another device: no remote copies, remote signals or barrier semaphores. Data moves between devices by JAX's collectives and lax.ppermute only.
A program may use at most 192 MiB of HBM per device.

```python
import math
import jax
import jax.numpy as jnp
import numpy as np
from jax import lax

D = 1536
HEADS = 24
KVH = 8
HD = 64
F = 512
TOP = 8
BLK = 256
EXPERTS = 16
SEQ = 1024
SEQS = 8
CAP = 160
N_CTX = 4


def draw_w_qkv(key, part):
    width_q = HEADS * HD
    width_k = KVH * HD
    base = jax.random.normal(key, (D, width_q + 2 * width_k), jnp.float32) * D ** (-0.5)
    return jnp.clip(base, -1.0, 1.0).astype(jnp.bfloat16)


def spiked(drawn, own_key, source, target, shards_of, factor):
    def block_of(position):
        return (jnp.arange(drawn.shape[position]) // (drawn.shape[position] // shards_of)).reshape((-1,) + (1,) * (drawn.ndim - 1 - position))

    first = jax.random.permutation(own_key, shards_of)[block_of(target)]
    other_side = (block_of(target) + shards_of // 2) % shards_of
    return jnp.where((block_of(source) == first) | (block_of(source) == other_side), factor * drawn, drawn)


def level_of(own_key, extent, cuts, least, largest):
    loudness = 1.0
    for position, blocks in cuts:
        draws = jax.random.uniform(jax.random.fold_in(jax.random.fold_in(own_key, 6), position), (blocks,), jnp.float32, least / len(cuts), largest / len(cuts))
        loudness = loudness * jnp.repeat(jnp.exp(draws), extent[position] // blocks).reshape((-1,) + (1,) * (len(extent) - 1 - position))
    return loudness


def shared_out(rng, own, number, rows, count, top, most, skew):
    order = jax.random.permutation(rng, count)
    crowded, ordinary = portions_of(count, rows * top, most, skew, True), portions_of(count, rows * top, most, skew, False)
    places = jnp.arange(count)

    def named(tallies, rotation):
        used = int((tallies > 0).sum())
        fixed = max(1, used // 4)
        passed = fixed + (places - fixed + rotation * (used - fixed)) % max(1, count - fixed)
        return jnp.zeros((count,), jnp.int32).at[order[jnp.where(places < fixed, places, passed)]].set(jnp.asarray(tallies, jnp.int32))

    tallies = jnp.where(number % 4 == 0, named(crowded, number // 4), named(ordinary, number - number // 4 - 1))
    mixed = jax.random.permutation(jax.random.fold_in(own, 3), count)
    giver, sink = mixed[0:count // 2 * 2:2], mixed[1:count // 2 * 2:2]
    slack = jnp.minimum(tallies[giver] - 1, most - tallies[sink]) // 2
    slack = jnp.where((giver == order[0]) | (sink == order[0]) | (tallies[sink] == 0), 0, jnp.maximum(slack, 0))
    passed = jax.random.randint(jax.random.fold_in(own, 4), (count // 2,), 0, 1 << 20) % (slack + 1)
    tallies = tallies.at[giver].add(-passed).at[sink].add(passed)
    labels = jnp.searchsorted(jnp.cumsum(tallies), jnp.arange(rows * top), side="right").astype(jnp.int32)
    grid = labels.reshape(top, rows).T
    grid = grid[jax.random.permutation(jax.random.fold_in(own, 1), rows)]
    rotation = jax.random.randint(jax.random.fold_in(own, 2), (rows, 1), 0, top)
    return jnp.take_along_axis(grid, (jnp.arange(top)[None, :] + rotation) % top, axis=1)


def portions_of(number_of, total, bound, skew, full):
    portions = [(1 << 20) // math.isqrt(grade ** skew) + 1 for grade in range(1, number_of + 1)]
    largest = bound if full else min(bound, max(-(-total // number_of), total * portions[0] // sum(portions)))
    least = 1 if total - largest >= number_of - 1 else 0
    counts, surplus = [largest] + [least] * (number_of - 1), total - largest - least * (number_of - 1)
    while surplus > 0:
        free = [i for i in range(1, number_of) if counts[i] < largest] or [i for i in range(1, number_of) if counts[i] < bound]
        pool, budget = sum([portions[i] for i in free]), surplus
        for i in free:
            extra = min(bound - counts[i], max(1, budget * portions[i] // pool), surplus)
            counts[i] = counts[i] + extra
            surplus = surplus - extra
    return np.array(counts)


def noise(own_key, extent, deviation, bound, split=(), held_as=jnp.bfloat16):
    gain = level_of(own_key, extent, split, -0.22, 0.18) if split else 1.0
    array = jax.random.normal(own_key, extent, jnp.float32) * deviation * gain
    return jnp.minimum(jnp.maximum(array, -bound), bound).astype(held_as)


def bell_draw_with(key, extent, spread, limit, shards, heavy, kind=jnp.bfloat16):
    array = spread * jax.random.normal(key, extent, jnp.float32)
    if shards:
        array = array * level_of(key, extent, shards, -0.22, 0.18)
    return jnp.clip(spiked(array, jax.random.fold_in(key, 3), *heavy), -limit, limit).astype(kind)


def setup_inputs(seed: int = 0) -> dict:
    seeds = jax.random.split(jax.random.key(seed), 11)
    hidden_in = bell_draw_with(seeds[0], (SEQS, SEQ, D), 1.0, 6.0, ((0, 8), (1, 4)), (0, 2, 8, 2.0))
    norm_attn = jnp.clip(1.0 + 0.1 * jax.random.normal(seeds[1], (D,), jnp.float32), 0.5, 1.5).astype(jnp.bfloat16)
    w_qkv = draw_w_qkv(jax.random.fold_in(seeds[10], 71), 0)
    w_mix = noise(seeds[3], (HEADS * HD, D), (max(D // 256, 1)) ** -0.5, 2.5, ((0, 8),))
    norm_moe = jnp.clip(1.0 + 0.1 * jax.random.normal(seeds[4], (D,), jnp.float32), 0.5, 1.5).astype(jnp.bfloat16)
    w_in = noise(seeds[5], (EXPERTS, D, 2 * F), D ** -0.5, 0.15625, ((0, 8),))
    w_out = noise(seeds[6], (EXPERTS, D, F), (F // 16) ** -0.5, 1.0, ((0, 8),))
    routes_keys = jax.random.split(jax.random.fold_in(seeds[7], 1), SEQS * SEQ // BLK)
    routes_turns = jax.random.permutation(jax.random.fold_in(seeds[7], 3), SEQS * SEQ // BLK)
    routes = jax.vmap(lambda own, number: shared_out(jax.random.fold_in(seeds[7], 2), own, number, BLK, EXPERTS, TOP, CAP, 1))(routes_keys, routes_turns).reshape((SEQS, SEQ, TOP))
    gates = jnp.clip(jnp.exp(math.log(0.5) - 2.3025851 * jax.random.uniform(seeds[8], (SEQS, SEQ, TOP), jnp.float32) ** level_of(seeds[8], (SEQS, SEQ, TOP), ((0, 8), (1, 4)), -0.2, 0.2)), 0.05, 0.5)
    cotangent = noise(seeds[9], (SEQS, SEQ, D), 1.0, 6.0, ((0, 8), (1, 4)))
    return {"hidden_in": hidden_in, "norm_attn": norm_attn, "w_qkv": w_qkv, "w_mix": w_mix, "norm_moe": norm_moe, "w_in": w_in, "w_out": w_out, "routes": routes, "gates": gates, "cotangent": cotangent}


@jax.custom_vjp
def low(v):
    return lax.optimization_barrier(v.astype(jnp.bfloat16)).astype(jnp.float32)

@jax.custom_vjp
def low_back(v):
    return v

def low_keep(v):
    return (low(v), None)

def low_pass(kept, grad):
    return (grad,)

def back_keep(v):
    return (v, None)

def back_low(kept, grad):
    return (low(grad),)
low.defvjp(low_keep, low_pass)
low_back.defvjp(back_keep, back_low)

def rms_scale(values):
    return lax.rsqrt(lax.optimization_barrier(jnp.mean(values * values, axis=-1, keepdims=True)) + 1e-05)

def rotate(values, positions, turn_sign):
    half_width = values.shape[-1] // 2
    frequency = 10000.0 ** (-jnp.arange(half_width, dtype=jnp.float32) / half_width)
    angles = positions.astype(jnp.float32)[:, None] * frequency[None, :]
    target_shape = (angles.shape[0],) + (1,) * (values.ndim - 2) + (half_width,)
    cosine = jnp.cos(angles).reshape(target_shape)
    sine_part = turn_sign * jnp.sin(angles).reshape(target_shape)
    leading = values[..., :half_width]
    trailing = values[..., half_width:]
    return jnp.concatenate([leading * cosine - trailing * sine_part, trailing * cosine + leading * sine_part], axis=-1)

def attend_block(query_block, block_start, key_rows, value_rows):
    raw_scores = jnp.einsum('qgrd,kgd->grqk', query_block, key_rows, precision=lax.Precision.HIGHEST)
    logits = low_back(raw_scores) * HD ** (-0.5)
    query_pos = block_start + jnp.arange(query_block.shape[0], dtype=jnp.int32)
    columns = jnp.arange(key_rows.shape[0], dtype=jnp.int32)
    logits = jnp.where(columns[None, :] <= query_pos[:, None], logits, -1e+30)
    weights = jax.nn.softmax(logits, axis=-1)
    return jnp.einsum('grqk,kgd->qgrd', low(weights), value_rows, precision=lax.Precision.HIGHEST)

def attention_part(sequence, gain_attn, w_qkv, w_mix):
    length = sequence.shape[0]
    positions = jnp.arange(length, dtype=jnp.int32)
    normed = low(sequence * rms_scale(sequence) * gain_attn)
    projected = low_back(jnp.dot(normed, w_qkv, precision=lax.Precision.HIGHEST, preferred_element_type=jnp.float32))
    group_size = HEADS // KVH
    width_q = HEADS * HD
    width_k = KVH * HD
    query = projected[:, :width_q].reshape(length, KVH, group_size, HD)
    key_rows = projected[:, width_q:width_q + width_k].reshape(length, KVH, HD)
    value_rows = low(projected[:, width_q + width_k:].reshape(length, KVH, HD))
    query = low(rotate(query, positions, 1.0))
    key_rows = low(rotate(key_rows, positions, 1.0))
    block_size = min(512, length)
    block_count = length // block_size
    blocks = query.reshape(block_count, block_size, KVH, group_size, HD)
    starts = jnp.arange(block_count, dtype=jnp.int32) * block_size
    attend = jax.checkpoint(lambda pieces: attend_block(pieces[0], pieces[1], key_rows, value_rows))
    attended = lax.map(attend, (blocks, starts)).reshape(length, width_q)
    mixed = low(low_back(attended))
    branch = low_back(jnp.dot(mixed, w_mix, precision=lax.Precision.HIGHEST, preferred_element_type=jnp.float32))
    return sequence + branch

def moe_block(pieces, gain_moe, w_in, w_out):
    block_vals, route_block, gate_block = pieces
    normed = low(block_vals * rms_scale(block_vals) * gain_moe)
    flat_routes = route_block.reshape(-1).astype(jnp.int32)
    onehot = (flat_routes[:, None] == jnp.arange(EXPERTS, dtype=jnp.int32)[None, :]).astype(jnp.int32)
    slots = (lax.optimization_barrier(jnp.sum(jnp.cumsum(onehot, axis=0) * onehot, axis=1)) - 1).astype(jnp.int32)
    tokens_of = jnp.arange(BLK * TOP, dtype=jnp.int32) // TOP
    buffer = jnp.zeros((EXPERTS, CAP, D), jnp.float32).at[flat_routes, slots].set(normed[tokens_of])
    dispatched = low_back(buffer)
    paired = low_back(jnp.einsum('ecd,edf->ecf', dispatched, w_in, precision=lax.Precision.HIGHEST))
    gate_part = paired[..., :F]
    up_part = paired[..., F:]
    hidden = low(jax.nn.silu(gate_part) * up_part)
    result = low(low_back(jnp.einsum('ecf,edf->ecd', hidden, w_out, precision=lax.Precision.HIGHEST)))
    picked = result[flat_routes, slots].reshape(BLK, TOP, D)
    return block_vals + lax.optimization_barrier(jnp.sum(picked * gate_block[:, :, None], axis=1))

def reference(hidden_in, norm_attn, w_qkv, w_mix, norm_moe, w_in, w_out, routes, gates, cotangent):
    primals = (hidden_in.astype(jnp.float32), norm_attn.astype(jnp.float32), w_qkv.astype(jnp.float32), w_mix.astype(jnp.float32), norm_moe.astype(jnp.float32), w_in.astype(jnp.float32), w_out.astype(jnp.float32), gates.astype(jnp.float32))

    def forward(inputs, gain_one, proj_qkv, proj_mix, gain_two, expert_in, expert_out, gate_vals):
        attention = jax.checkpoint(lambda sequence: attention_part(sequence, gain_one, proj_qkv, proj_mix))
        middle = lax.map(attention, inputs)
        block_count = middle.shape[0] * N_CTX
        block_in = (middle.reshape(block_count, BLK, D), routes.reshape(block_count, BLK, TOP), gate_vals.reshape(block_count, BLK, TOP))
        expert_fn = jax.checkpoint(lambda pieces: moe_block(pieces, gain_two, expert_in, expert_out))
        return lax.map(expert_fn, block_in).reshape(middle.shape)
    layer_out, pullback = jax.vjp(forward, *primals)
    gradients = pullback(cotangent.astype(jnp.float32))
    return (layer_out.astype(jnp.bfloat16), gradients[0], gradients[1], gradients[2], gradients[3], gradients[4], gradients[5], gradients[6], gradients[7])
```

```python
import functools

import jax
import jax.numpy as jnp
from jax import lax
from jax.experimental import pallas as pl
from jax.experimental.pallas import tpu as pltpu
from jax.sharding import PartitionSpec as P

HEADS = 24
KVH = 8
HD = 64
F = 512
TOP = 8
EPS = 1e-05
F32 = jnp.float32
BF16 = jnp.bfloat16


def rms_scale(values):
    return lax.rsqrt(jnp.mean(values * values, axis=-1, keepdims=True) + EPS)


def pad_to(width, unit):
    return -(-width // unit) * unit


def pad_cols(array, width):
    if array.shape[1] == width:
        return array
    return jnp.pad(array, ((0, 0), (0, width - array.shape[1])))


def swap_halves(values):
    lane = lax.broadcasted_iota(jnp.int32, values.shape, 1)
    return jnp.where(
        lane % HD < HD // 2,
        pltpu.roll(values, values.shape[1] - HD // 2, 1),
        pltpu.roll(values, HD // 2, 1),
    )


def turn(values, cosine, sine, sign):
    pieces = []
    for start in range(0, values.shape[1], 128):
        tile = values[:, start : start + 128]
        pieces.append(tile * cosine + sign * (swap_halves(tile) * sine))
    return pieces[0] if len(pieces) == 1 else jnp.concatenate(pieces, axis=1)


def qkv_kernel(widths, x_ref, gain_ref, w_ref, cos_ref, sin_ref, a_ref, q_ref, k_ref, v_ref):
    wq, wk, wv = widths
    x = x_ref[...].astype(F32)
    scale = lax.rsqrt(jnp.mean(x * x, axis=1, keepdims=True) + EPS)
    a = (x * scale * gain_ref[...]).astype(BF16)
    a_ref[...] = a
    proj = jnp.dot(a, w_ref[...], preferred_element_type=F32)
    cosine = cos_ref[...]
    sine = sin_ref[...]
    q_ref[...] = turn(proj[:, :wq], cosine, sine, 1.0).astype(BF16)
    k_ref[...] = turn(proj[:, wq : wq + wk], cosine, sine, 1.0).astype(BF16)
    v_ref[...] = proj[:, wq + wk :].astype(BF16)


def nt(left, right):
    return lax.dot_general(left, right, (((1,), (1,)), ((), ())), preferred_element_type=F32)


def tn(left, right):
    return lax.dot_general(left, right, (((0,), (0,)), ((), ())), preferred_element_type=F32)


def causal(keys, rows, start):
    key = lax.broadcasted_iota(jnp.int32, (keys, rows), 0)
    query = lax.broadcasted_iota(jnp.int32, (keys, rows), 1) + start
    return key <= query


def attend_kernel(blocks, rows, kv_heads, group, q_ref, k_ref, v_ref, o_ref, l_ref):
    step = pl.program_id(0)
    for block in range(blocks):

        @pl.when(step == block)
        def _(block=block):
            keys = (block + 1) * rows
            allowed = causal(keys, rows, block * rows)
            l_ref[...] = jnp.zeros_like(l_ref)
            for g in range(kv_heads):
                key = k_ref[:keys, g * HD : (g + 1) * HD]
                value = v_ref[:keys, g * HD : (g + 1) * HD]
                for r in range(group):
                    h = g * group + r
                    query = q_ref[:, h * HD : (h + 1) * HD]
                    scores = jnp.where(allowed, nt(key, query) * HD**-0.5, -1e30)
                    top = jnp.max(scores, axis=0, keepdims=True)
                    weights = jnp.exp(scores - top)
                    total = jnp.sum(weights, axis=0, keepdims=True)
                    out = tn(value, weights.astype(BF16)) / total
                    o_ref[:, h * HD : (h + 1) * HD] = out.T.astype(BF16)
                    l_ref[0, h : h + 1, :] = top + jnp.log(total)


def attend_back_kernel(
    blocks, rows, kv_heads, group, q_ref, k_ref, v_ref, d_ref, l_ref, cosq_ref, sinq_ref,
    cos_ref, sin_ref, dq_ref, dkv_ref, dk_acc, dv_acc, dq_acc,
):
    step = pl.program_id(0)

    @pl.when(step == 0)
    def _():
        dk_acc[...] = jnp.zeros_like(dk_acc)
        dv_acc[...] = jnp.zeros_like(dv_acc)
        dq_acc[...] = jnp.zeros_like(dq_acc)

    for block in range(blocks):

        @pl.when(step == block)
        def _(block=block):
            keys = (block + 1) * rows
            allowed = causal(keys, rows, block * rows)
            for g in range(kv_heads):
                lanes = slice(g * HD, (g + 1) * HD)
                key = k_ref[:keys, lanes]
                value = v_ref[:keys, lanes]
                dk = None
                dv = None
                for r in range(group):
                    h = g * group + r
                    query = q_ref[:, h * HD : (h + 1) * HD]
                    d_out = d_ref[:, h * HD : (h + 1) * HD]
                    scores = jnp.where(allowed, nt(key, query) * HD**-0.5, -1e30)
                    weights = jnp.exp(scores - l_ref[0, h : h + 1, :])
                    d_weights = nt(value, d_out)
                    delta = jnp.sum(weights * d_weights, axis=0, keepdims=True)
                    d_scores = (HD**-0.5 * weights * (d_weights - delta)).astype(BF16)
                    dq_acc[:, h * HD : (h + 1) * HD] = tn(key, d_scores).T
                    dk_part = jnp.dot(d_scores, query, preferred_element_type=F32)
                    dv_part = jnp.dot(weights.astype(BF16), d_out, preferred_element_type=F32)
                    dk = dk_part if dk is None else dk + dk_part
                    dv = dv_part if dv is None else dv + dv_part
                dk_acc[:keys, lanes] += dk
                dv_acc[:keys, lanes] += dv

    dq_ref[...] = turn(dq_acc[...], cosq_ref[...], sinq_ref[...], -1.0).astype(BF16)

    @pl.when(step == blocks - 1)
    def _():
        wk = dk_acc.shape[1]
        dkv_ref[:, :wk] = turn(dk_acc[...], cos_ref[...], sin_ref[...], -1.0).astype(BF16)
        dkv_ref[:, wk:] = dv_acc[...].astype(BF16)


def row_block(rows, width):
    return pl.BlockSpec((rows, width), lambda i: (i, 0))


def whole_block(*shape):
    return pl.BlockSpec(shape, lambda i: (0,) * len(shape))


def local(hidden_in, norm_attn, w_qkv, w_mix, norm_moe, w_in, w_out, routes, gates, cotangent):
    groups = lax.axis_size("fsdp")
    ctx = lax.axis_size("ctx")
    here = lax.axis_index("ctx")
    shard = lax.axis_index("fsdp")
    rows = hidden_in.shape[1]
    width = hidden_in.shape[2]
    seq = rows * ctx
    group = HEADS // KVH
    kv_heads = KVH // ctx
    q_real, k_real = kv_heads * group * HD, kv_heads * HD
    wq, wk = pad_to(q_real, 128), pad_to(k_real, 128)
    proj_cols = wq + 2 * wk
    per_expert = w_in.shape[0]
    experts = per_expert * groups
    capacity = 5 * rows * TOP // (4 * experts)
    shard_rows = w_qkv.shape[0]

    def partner(array, s):
        return lax.ppermute(array, "ctx", [(i, i ^ s) for i in range(ctx)])

    half = HD // 2
    frequency = 10000.0 ** (-jnp.arange(half, dtype=F32) / half)
    angles = jnp.arange(seq, dtype=jnp.int32).astype(F32)[:, None] * frequency[None, :]
    cos_half, sin_half = jnp.cos(angles), jnp.sin(angles)
    cos_table = jnp.concatenate([cos_half] * 4, axis=1)
    sin_table = jnp.concatenate([-sin_half, sin_half] * 2, axis=1)

    own = hidden_in[0]
    x_all = jnp.zeros((ctx, rows, width), BF16)
    for s in range(ctx):
        x_all = lax.dynamic_update_index_in_dim(
            x_all, own if s == 0 else partner(own, s), here ^ s, 0
        )
    x_all = x_all.reshape(seq, width)

    def columns_of(matrix):
        return jnp.concatenate(
            [
                pad_cols(lax.dynamic_slice_in_dim(matrix, here * q_real, q_real, 1), wq),
                pad_cols(lax.dynamic_slice_in_dim(matrix, HEADS * HD + here * k_real, k_real, 1), wk),
                pad_cols(
                    lax.dynamic_slice_in_dim(matrix, (HEADS + KVH) * HD + here * k_real, k_real, 1), wk
                ),
            ],
            axis=1,
        )

    extra = 16
    gains = pad_cols(jnp.stack([norm_attn, norm_moe]), proj_cols)
    gains = jnp.pad(gains, ((0, extra - 2), (0, 0)))
    gathered = lax.all_gather(
        jnp.concatenate([columns_of(w_qkv), gains], axis=0), "fsdp", axis=0, tiled=False
    )
    head_w = gathered[:, :shard_rows].reshape(width, proj_cols)
    gain_one = gathered[:, shard_rows, :shard_rows].reshape(1, width).astype(F32)
    gain_two = gathered[:, shard_rows + 1, :shard_rows].reshape(1, width).astype(F32)
    full_mix = lax.all_gather(w_mix, "fsdp", axis=0, tiled=True)

    expert_ids = jnp.arange(experts, dtype=jnp.int32)
    named = routes[0][None, :, :] == expert_ids[:, None, None]
    dense_gates = jnp.sum(jnp.where(named, gates[0][None, :, :], 0.0), axis=2)
    gate_rows = lax.all_to_all(dense_gates, "fsdp", split_axis=0, concat_axis=0, tiled=True)
    gate_rows = gate_rows.reshape(groups, per_expert, rows)

    a_all, query, keys, values = pl.pallas_call(
        functools.partial(qkv_kernel, (wq, wk, wk)),
        grid=(ctx,),
        in_specs=[
            row_block(rows, width),
            whole_block(1, width),
            whole_block(width, proj_cols),
            row_block(rows, 128),
            row_block(rows, 128),
        ],
        out_specs=[
            row_block(rows, width),
            row_block(rows, wq),
            row_block(rows, wk),
            row_block(rows, wk),
        ],
        out_shape=[
            jax.ShapeDtypeStruct((seq, width), BF16),
            jax.ShapeDtypeStruct((seq, wq), BF16),
            jax.ShapeDtypeStruct((seq, wk), BF16),
            jax.ShapeDtypeStruct((seq, wk), BF16),
        ],
        name="qkv",
    )(x_all, gain_one, head_w, cos_table, sin_table)

    heads = kv_heads * group
    mixed_heads, log_total = pl.pallas_call(
        functools.partial(attend_kernel, ctx, rows, kv_heads, group),
        grid=(ctx,),
        in_specs=[row_block(rows, wq), whole_block(seq, wk), whole_block(seq, wk)],
        out_specs=[row_block(rows, q_real), pl.BlockSpec((1, 8, rows), lambda i: (i, 0, 0))],
        out_shape=[
            jax.ShapeDtypeStruct((seq, q_real), BF16),
            jax.ShapeDtypeStruct((ctx, 8, rows), F32),
        ],
        name="attend",
    )(query, keys, values)

    mixed = jnp.zeros((rows, HEADS * HD), BF16)
    for s in range(ctx):
        piece = lax.dynamic_slice_in_dim(mixed_heads, (here ^ s) * rows, rows, 0)
        piece = piece if s == 0 else partner(piece, s)
        mixed = lax.dynamic_update_slice_in_dim(mixed, piece, (here ^ s) * q_real, 1)

    inputs = own.astype(F32)
    scale_one = rms_scale(inputs)
    unit_one = inputs * scale_one
    middle = inputs + jnp.dot(mixed, full_mix, preferred_element_type=F32)
    scale_two = rms_scale(middle)
    unit_two = middle * scale_two
    normed_two = (unit_two * gain_two).astype(BF16)

    tokens = lax.all_gather(normed_two, "fsdp", axis=0, tiled=False)
    cotangents = lax.all_gather(cotangent[0], "fsdp", axis=0, tiled=False)

    named_here = gate_rows > 0
    triangle = (
        jnp.arange(rows, dtype=jnp.int32)[:, None] <= jnp.arange(rows, dtype=jnp.int32)[None, :]
    ).astype(BF16)
    counts = jnp.einsum(
        "bet,tu->beu", named_here.astype(BF16), triangle, preferred_element_type=F32
    )
    slot_of = jnp.where(named_here, counts.astype(jnp.int32) - 1, -1)
    slot_ids = jnp.arange(capacity, dtype=jnp.int32)
    y_part = 0.0
    saved = []
    for e in range(per_expert):
        pick = slot_of[:, e, None, :] == slot_ids[None, :, None]
        gate_slot = jnp.sum(jnp.where(pick, gate_rows[:, e, None, :], 0.0), axis=2)
        pick = pick.astype(BF16)

        def to_slots(array, pick=pick):
            return (
                jnp.einsum("bst,btd->bsd", pick, array, preferred_element_type=F32)
                .astype(BF16)
                .reshape(groups * capacity, width)
            )

        gate_slot = gate_slot.reshape(groups * capacity, 1)
        arrived = to_slots(tokens)
        paired = jnp.dot(arrived, w_in[e], preferred_element_type=F32)
        gate_part, up_part = paired[:, :F], paired[:, F:]
        hidden = (jax.nn.silu(gate_part) * up_part).astype(BF16)
        result = lax.dot_general(
            hidden, w_out[e], (((1,), (1,)), ((), ())), preferred_element_type=F32
        )
        scaled = (result * gate_slot).astype(BF16).reshape(groups, capacity, width)
        y_part = y_part + jnp.einsum("bst,bsd->btd", pick, scaled, preferred_element_type=F32)
        saved.append((pick, to_slots, gate_slot, arrived, gate_part, up_part, hidden, result))
    y_sum = lax.psum_scatter(y_part.astype(BF16), "fsdp", scatter_dimension=0, tiled=False)

    db_part = 0.0
    gate_grads, grads_in, grads_out = [], [], []
    for e in range(per_expert):
        pick, to_slots, gate_slot, arrived, gate_part, up_part, hidden, result = saved[e]
        cot_rows = to_slots(cotangents).astype(F32)
        gate_grad_slot = jnp.sum(cot_rows * result, axis=1).reshape(groups, capacity, 1)
        gate_grads.append(jnp.sum(pick.astype(F32) * gate_grad_slot, axis=1))
        d_result = (cot_rows * gate_slot).astype(BF16)
        d_hidden = jnp.dot(d_result, w_out[e], preferred_element_type=F32)
        sigmoid_gate = jax.nn.sigmoid(gate_part)
        d_gate = d_hidden * up_part * sigmoid_gate * (1.0 + gate_part * (1.0 - sigmoid_gate))
        d_up = d_hidden * gate_part * sigmoid_gate
        d_paired = jnp.concatenate([d_gate, d_up], axis=-1).astype(BF16)
        d_rows = lax.dot_general(
            d_paired, w_in[e], (((1,), (1,)), ((), ())), preferred_element_type=F32
        )
        d_rows = d_rows.astype(BF16).reshape(groups, capacity, width)
        db_part = db_part + jnp.einsum("bst,bsd->btd", pick, d_rows, preferred_element_type=F32)
        grads_in.append(
            lax.dot_general(
                arrived, d_paired, (((0,), (0,)), ((), ())), preferred_element_type=F32
            ).astype(BF16)
        )
        grads_out.append(
            lax.dot_general(
                d_result, hidden, (((0,), (0,)), ((), ())), preferred_element_type=F32
            ).astype(BF16)
        )
    d_normed_two = lax.psum_scatter(
        db_part.astype(BF16), "fsdp", scatter_dimension=0, tiled=False
    ).astype(F32)

    gate_grad = jnp.stack(gate_grads, axis=1).reshape(groups * per_expert, rows)
    gate_grad = lax.all_to_all(gate_grad, "fsdp", split_axis=0, concat_axis=0, tiled=True)
    gate_grad = jnp.sum(jnp.where(named, gate_grad[:, :, None], 0.0), axis=0)

    grad_in_part, grad_out_part = (
        lax.psum_scatter(jnp.stack(grads_in), "ctx", scatter_dimension=1, tiled=True).astype(F32),
        lax.psum_scatter(jnp.stack(grads_out), "ctx", scatter_dimension=1, tiled=True).astype(F32),
    )

    grad_out = cotangent[0].astype(F32)
    outputs = middle + y_sum.astype(F32)
    grad_gain_two = jnp.sum(d_normed_two * unit_two, axis=0)
    scaled_two = d_normed_two * gain_two
    d_middle = grad_out + scale_two * (
        scaled_two - unit_two * jnp.mean(scaled_two * unit_two, axis=-1, keepdims=True)
    )
    d_branch = d_middle.astype(BF16)
    d_mixed = lax.dot_general(
        d_branch, full_mix, (((1,), (1,)), ((), ())), preferred_element_type=F32
    ).astype(BF16)
    d_heads = jnp.zeros((ctx, rows, q_real), BF16)
    for s in range(ctx):
        piece = lax.dynamic_slice_in_dim(d_mixed, (here ^ s) * q_real, q_real, 1)
        piece = piece if s == 0 else partner(piece, s)
        d_heads = lax.dynamic_update_index_in_dim(d_heads, piece, here ^ s, 0)
    d_heads = d_heads.reshape(seq, q_real)

    grad_mix_local = lax.dot_general(
        mixed, d_branch, (((0,), (0,)), ((), ())), preferred_element_type=F32
    )
    mix_cols = width // ctx

    d_query, d_keys_values = pl.pallas_call(
        functools.partial(attend_back_kernel, ctx, rows, kv_heads, group),
        grid=(ctx,),
        in_specs=[
            row_block(rows, wq),
            whole_block(seq, wk),
            whole_block(seq, wk),
            row_block(rows, q_real),
            pl.BlockSpec((1, 8, rows), lambda i: (i, 0, 0)),
            row_block(rows, 128),
            row_block(rows, 128),
            whole_block(seq, 128),
            whole_block(seq, 128),
        ],
        out_specs=[row_block(rows, wq), whole_block(seq, 2 * wk)],
        out_shape=[
            jax.ShapeDtypeStruct((seq, wq), BF16),
            jax.ShapeDtypeStruct((seq, 2 * wk), BF16),
        ],
        scratch_shapes=[
            pltpu.VMEM((seq, wk), F32),
            pltpu.VMEM((seq, wk), F32),
            pltpu.VMEM((rows, wq), F32),
        ],
        name="attend_back",
    )(query, keys, values, d_heads, log_total, cos_table, sin_table, cos_table, sin_table)
    d_projected = jnp.concatenate([d_query, d_keys_values], axis=1)

    d_normed_part = lax.dot_general(
        d_projected, head_w, (((1,), (1,)), ((), ())), preferred_element_type=F32
    ).astype(BF16)
    d_normed_one = 0.0
    for s in range(ctx):
        piece = lax.dynamic_slice_in_dim(d_normed_part, (here ^ s) * rows, rows, 0)
        piece = piece if s == 0 else partner(piece, s)
        d_normed_one = d_normed_one + piece.astype(F32)
    grad_gain_one = jnp.sum(d_normed_one * unit_one, axis=0)
    scaled_one = d_normed_one * gain_one
    d_inputs = d_middle + scale_one * (
        scaled_one - unit_one * jnp.mean(scaled_one * unit_one, axis=-1, keepdims=True)
    )

    grad_qkv_local = lax.dot_general(
        a_all, d_projected, (((0,), (0,)), ((), ())), preferred_element_type=F32
    ).astype(BF16)
    grad_mix_cols = 0.0
    for s in range(ctx):
        piece = lax.dynamic_slice_in_dim(grad_mix_local, (here ^ s) * mix_cols, mix_cols, 1)
        piece = piece if s == 0 else partner(piece.astype(BF16), s).astype(F32)
        grad_mix_cols = grad_mix_cols + piece
    mix_sum = lax.psum_scatter(
        grad_mix_cols.astype(BF16), "fsdp", scatter_dimension=0, tiled=True
    )
    gain_grads = jnp.stack([grad_gain_one, grad_gain_two], axis=0).astype(BF16)
    gain_grads = gain_grads.reshape(2, groups, shard_rows).transpose(1, 0, 2)
    gain_grads = jnp.pad(
        gain_grads, ((0, 0), (0, extra - 2), (0, proj_cols - shard_rows))
    )
    qkv_sum = lax.psum_scatter(
        jnp.concatenate([grad_qkv_local.reshape(groups, shard_rows, proj_cols), gain_grads], axis=1),
        "fsdp",
        scatter_dimension=0,
        tiled=False,
    )
    final = jnp.concatenate(
        [qkv_sum, jnp.pad(mix_sum, ((0, extra), (0, 0)))], axis=1
    )
    finals = jnp.zeros((ctx,) + final.shape, BF16)
    for s in range(ctx):
        finals = lax.dynamic_update_index_in_dim(
            finals, final if s == 0 else partner(final, s), here ^ s, 0
        )
    finals = finals.astype(F32)

    def side_by_side(start, size):
        piece = finals[:, :shard_rows, start : start + size]
        return piece.transpose(1, 0, 2).reshape(shard_rows, ctx * size)

    total_qkv = jnp.concatenate(
        [
            side_by_side(0, q_real),
            side_by_side(wq, k_real),
            side_by_side(wq + wk, k_real),
        ],
        axis=1,
    )
    total_mix = side_by_side(proj_cols, mix_cols)
    total_one = jnp.sum(finals[:, shard_rows, :shard_rows], axis=0)
    total_two = jnp.sum(finals[:, shard_rows + 1, :shard_rows], axis=0)
    return (
        outputs.astype(BF16)[None],
        d_inputs[None],
        total_one,
        total_qkv,
        total_mix,
        total_two,
        grad_in_part,
        grad_out_part,
        gate_grad[None],
    )


def solution(mesh):
    placed = (
        P("fsdp", "ctx", None),
        P("fsdp"),
        P("fsdp", None),
        P("fsdp", None),
        P("fsdp"),
        P("fsdp", None, None),
        P("fsdp", None, None),
        P("fsdp", "ctx", None),
        P("fsdp", "ctx", None),
        P("fsdp", "ctx", None),
    )
    return jax.shard_map(
        local,
        mesh=mesh,
        in_specs=placed,
        out_specs=(
            P("fsdp", "ctx", None),
            P("fsdp", "ctx", None),
            P("fsdp"),
            P("fsdp", None),
            P("fsdp", None),
            P("fsdp"),
            P("fsdp", "ctx", None),
            P("fsdp", "ctx", None),
            P("fsdp", "ctx", None),
        ),
        check_vma=False,
    )
```

```python
import functools

import jax
import jax.numpy as jnp
from jax import lax
from jax.experimental import pallas as pl
from jax.experimental.pallas import tpu as pltpu
from jax.sharding import PartitionSpec as P

HEADS = 24
KVH = 8
HD = 64
F = 512
TOP = 8
EPS = 1e-05
F32 = jnp.float32
BF16 = jnp.bfloat16


def rms_scale(values):
    return lax.rsqrt(jnp.mean(values * values, axis=-1, keepdims=True) + EPS)


def pad_to(width, unit):
    return -(-width // unit) * unit


def pad_cols(array, width):
    if array.shape[1] == width:
        return array
    return jnp.pad(array, ((0, 0), (0, width - array.shape[1])))


def swap_halves(values):
    lane = lax.broadcasted_iota(jnp.int32, values.shape, 1)
    return jnp.where(
        lane % HD < HD // 2,
        pltpu.roll(values, values.shape[1] - HD // 2, 1),
        pltpu.roll(values, HD // 2, 1),
    )


def turn(values, cosine, sine, sign):
    pieces = []
    for start in range(0, values.shape[1], 128):
        tile = values[:, start : start + 128]
        pieces.append(tile * cosine + sign * (swap_halves(tile) * sine))
    return pieces[0] if len(pieces) == 1 else jnp.concatenate(pieces, axis=1)


def qkv_kernel(widths, x_ref, gain_ref, w_ref, cos_ref, sin_ref, a_ref, q_ref, k_ref, v_ref):
    wq, wk, wv = widths
    x = x_ref[...].astype(F32)
    scale = lax.rsqrt(jnp.mean(x * x, axis=1, keepdims=True) + EPS)
    a = (x * scale * gain_ref[...]).astype(BF16)
    a_ref[...] = a
    proj = jnp.dot(a, w_ref[...], preferred_element_type=F32)
    cosine = cos_ref[...]
    sine = sin_ref[...]
    q_ref[...] = turn(proj[:, :wq], cosine, sine, 1.0).astype(BF16)
    k_ref[...] = turn(proj[:, wq : wq + wk], cosine, sine, 1.0).astype(BF16)
    v_ref[...] = proj[:, wq + wk :].astype(BF16)


def nt(left, right):
    return lax.dot_general(left, right, (((1,), (1,)), ((), ())), preferred_element_type=F32)


def tn(left, right):
    return lax.dot_general(left, right, (((0,), (0,)), ((), ())), preferred_element_type=F32)


def causal(keys, rows, start):
    key = lax.broadcasted_iota(jnp.int32, (keys, rows), 0)
    query = lax.broadcasted_iota(jnp.int32, (keys, rows), 1) + start
    return key <= query


def attend_kernel(blocks, rows, kv_heads, group, q_ref, k_ref, v_ref, o_ref, l_ref):
    step = pl.program_id(0)
    for block in range(blocks):

        @pl.when(step == block)
        def _(block=block):
            keys = (block + 1) * rows
            allowed = causal(keys, rows, block * rows)
            l_ref[...] = jnp.zeros_like(l_ref)
            for g in range(kv_heads):
                key = k_ref[:keys, g * HD : (g + 1) * HD]
                value = v_ref[:keys, g * HD : (g + 1) * HD]
                for r in range(group):
                    h = g * group + r
                    query = q_ref[:, h * HD : (h + 1) * HD]
                    scores = jnp.where(allowed, nt(key, query) * HD**-0.5, -1e30)
                    top = jnp.max(scores, axis=0, keepdims=True)
                    weights = jnp.exp(scores - top)
                    total = jnp.sum(weights, axis=0, keepdims=True)
                    out = tn(value, weights.astype(BF16)) / total
                    o_ref[:, h * HD : (h + 1) * HD] = out.T.astype(BF16)
                    l_ref[0, h : h + 1, :] = top + jnp.log(total)


def attend_back_kernel(
    blocks, rows, kv_heads, group, q_ref, k_ref, v_ref, d_ref, l_ref, cosq_ref, sinq_ref,
    cos_ref, sin_ref, dq_ref, dkv_ref, dk_acc, dv_acc, dq_acc,
):
    step = pl.program_id(0)

    @pl.when(step == 0)
    def _():
        dk_acc[...] = jnp.zeros_like(dk_acc)
        dv_acc[...] = jnp.zeros_like(dv_acc)
        dq_acc[...] = jnp.zeros_like(dq_acc)

    for block in range(blocks):

        @pl.when(step == block)
        def _(block=block):
            keys = (block + 1) * rows
            allowed = causal(keys, rows, block * rows)
            for g in range(kv_heads):
                lanes = slice(g * HD, (g + 1) * HD)
                key = k_ref[:keys, lanes]
                value = v_ref[:keys, lanes]
                dk = None
                dv = None
                for r in range(group):
                    h = g * group + r
                    query = q_ref[:, h * HD : (h + 1) * HD]
                    d_out = d_ref[:, h * HD : (h + 1) * HD]
                    scores = jnp.where(allowed, nt(key, query) * HD**-0.5, -1e30)
                    weights = jnp.exp(scores - l_ref[0, h : h + 1, :])
                    d_weights = nt(value, d_out)
                    delta = jnp.sum(weights * d_weights, axis=0, keepdims=True)
                    d_scores = (HD**-0.5 * weights * (d_weights - delta)).astype(BF16)
                    dq_acc[:, h * HD : (h + 1) * HD] = tn(key, d_scores).T
                    dk_part = jnp.dot(d_scores, query, preferred_element_type=F32)
                    dv_part = jnp.dot(weights.astype(BF16), d_out, preferred_element_type=F32)
                    dk = dk_part if dk is None else dk + dk_part
                    dv = dv_part if dv is None else dv + dv_part
                dk_acc[:keys, lanes] += dk
                dv_acc[:keys, lanes] += dv

    dq_ref[...] = turn(dq_acc[...], cosq_ref[...], sinq_ref[...], -1.0).astype(BF16)

    @pl.when(step == blocks - 1)
    def _():
        wk = dk_acc.shape[1]
        dkv_ref[:, :wk] = turn(dk_acc[...], cos_ref[...], sin_ref[...], -1.0).astype(BF16)
        dkv_ref[:, wk:] = dv_acc[...].astype(BF16)


def mm(left, right):
    return jnp.dot(left, right, preferred_element_type=F32)


def expert_kernel(dims, place_ref, slot_ref, gate_ref, b0_ref, b1_ref, g_ref, win_ref, wout_ref, *refs):
    rows, capacity, units, with_saved = dims
    refs = refs[6:] if with_saved else refs
    y_ref, gg_ref, x_ref, r_ref, h_ref, p_ref, db0_ref, db1_ref, y_acc, db_acc = refs
    e = pl.program_id(0)
    core = place_ref[1]
    b_refs = (b0_ref, b1_ref)
    slots = lax.broadcasted_iota(jnp.int32, (capacity, rows), 0)
    picks, gate_cols = [], []
    for k in range(2):
        pick = slots == slot_ref[0, 0, k : k + 1, :]
        gate_cols.append(
            jnp.sum(jnp.where(pick, gate_ref[0, 0, k : k + 1, :], 0.0), axis=1, keepdims=True)
        )
        picks.append(pick.astype(F32).astype(BF16))
        x_ref[0, k * capacity : (k + 1) * capacity, :] = mm(picks[k], b_refs[k][...]).astype(BF16)
    win = win_ref[0]
    wout = wout_ref[0]
    paired = mm(x_ref[0], win)
    gate_part, up_part = paired[:, :units], paired[:, units:]
    sig = jax.nn.sigmoid(gate_part)
    silu = gate_part * sig
    hidden = (silu * up_part).astype(BF16)
    h_ref[0] = hidden
    result = nt(hidden, wout)
    gate_grads = []
    for k in range(2):
        part = slice(k * capacity, (k + 1) * capacity)
        cot = mm(picks[k], g_ref[0, core ^ k])
        r_ref[0, part, :] = (cot * gate_cols[k]).astype(BF16)
        gate_grad = jnp.sum(cot * result[part], axis=1, keepdims=True)
        gate_grads.append(jnp.sum(picks[k].astype(F32) * gate_grad, axis=0, keepdims=True))
        y_part = tn(picks[k], (result[part] * gate_cols[k]).astype(BF16))
        y_acc[k] = jnp.where(e == 0, y_part, y_acc[k] + y_part)
    gg_ref[0, 0] = jnp.where(
        core == 0,
        jnp.concatenate(gate_grads, axis=0),
        jnp.concatenate(gate_grads[::-1], axis=0),
    )
    d_hidden = mm(r_ref[0], wout)
    d_gate = d_hidden * up_part * sig * (1.0 + gate_part * (1.0 - sig))
    d_up = d_hidden * silu
    p_ref[0, :, :units] = d_gate.astype(BF16)
    p_ref[0, :, units:] = d_up.astype(BF16)
    d_rows = nt(p_ref[0], win).astype(BF16)
    for k in range(2):
        db_part = tn(picks[k], d_rows[k * capacity : (k + 1) * capacity])
        db_acc[k] = jnp.where(e == 0, db_part, db_acc[k] + db_part)

    @pl.when(e == pl.num_programs(0) - 1)
    def _():
        for k in range(2):
            y_ref[0, core ^ k] = y_acc[k].astype(BF16)
        db0_ref[...] = db_acc[0].astype(BF16)
        db1_ref[...] = db_acc[1].astype(BF16)


def experts_unit(place, slot, gate, b_pair, g, w_in, w_out, capacity, unit, saved):
    per_expert, width, double = w_in.shape
    units = w_out.shape[2]
    ring, _, rows, _ = g.shape
    slots = 2 * capacity
    widths = (width, width, units, 2 * units)
    per_e = lambda *s: pl.BlockSpec((1,) + s, lambda e, p: (e,) + (0,) * len(s))
    whole = lambda *s: pl.BlockSpec(s, lambda e, p: (0,) * len(s))
    token_spec = pl.BlockSpec((1, 2, rows, width), lambda e, p: (p[0], 0, 0, 0))
    gate_spec = pl.BlockSpec((1, 1, 2, rows), lambda e, p: (unit, e, 0, 0))
    in_specs = [gate_spec, gate_spec, whole(rows, width), whole(rows, width), token_spec]
    in_specs += [per_e(width, double), per_e(width, units)]
    args = [place, slot, gate, *b_pair, g, w_in, w_out]
    aliases = {}
    if saved is not None:
        in_specs += [pl.BlockSpec(memory_space=pl.ANY)] * 6
        args += list(saved)
        aliases = {8 + i: i for i in range(6)}
    out = pl.pallas_call(
        functools.partial(expert_kernel, (rows, capacity, units, saved is not None)),
        grid_spec=pltpu.PrefetchScalarGridSpec(
            num_scalar_prefetch=1,
            grid=(per_expert,),
            in_specs=in_specs,
            out_specs=[
                token_spec,
                pl.BlockSpec((1, 1, 2, rows), lambda e, p: (p[0], e, 0, 0)),
                *[pl.BlockSpec((1, slots, w), lambda e, p: (e, unit, 0)) for w in widths],
                whole(rows, width),
                whole(rows, width),
            ],
            scratch_shapes=[pltpu.VMEM((2, rows, width), F32)] * 2,
        ),
        out_shape=[
            jax.ShapeDtypeStruct(g.shape, BF16),
            jax.ShapeDtypeStruct((ring, per_expert, 2, rows), F32),
            *[jax.ShapeDtypeStruct((per_expert, ring * slots, w), BF16) for w in widths],
            jax.ShapeDtypeStruct((rows, width), BF16),
            jax.ShapeDtypeStruct((rows, width), BF16),
        ],
        input_output_aliases=aliases,
        compiler_params=pltpu.CompilerParams(vmem_limit_bytes=56 * 2**20),
        name="experts",
    )(*args)
    return out[:6], out[6], out[7]


def weight_kernel(cols_in, x_ref, p_ref, r_ref, h_ref, o_ref):
    o_ref[:, :cols_in] = tn(x_ref[0], p_ref[0]).astype(BF16)
    o_ref[:, cols_in:] = tn(r_ref[0], h_ref[0]).astype(BF16)


def weight_grads(saved, e, tile):
    x, r, h, p = saved
    _, total, width = x.shape
    units = h.shape[2]
    tiled = pl.BlockSpec((1, total, tile), lambda i: (e, 0, i))
    return pl.pallas_call(
        functools.partial(weight_kernel, 2 * units),
        grid=(width // tile,),
        in_specs=[
            tiled,
            pl.BlockSpec((1, total, 2 * units), lambda i: (e, 0, 0)),
            tiled,
            pl.BlockSpec((1, total, units), lambda i: (e, 0, 0)),
        ],
        out_specs=pl.BlockSpec((tile, 3 * units), lambda i: (i, 0)),
        out_shape=jax.ShapeDtypeStruct((width, 3 * units), BF16),
        compiler_params=pltpu.CompilerParams(vmem_limit_bytes=56 * 2**20),
        name="weight_grads",
    )(x, p, r, h)


def input_grad_kernel(dq_ref, dkv_ref, w_ref, x_ref, o_ref, g_ref):
    wq = dq_ref.shape[1]
    part = nt(dq_ref[...], w_ref[:, :wq]) + nt(dkv_ref[...], w_ref[:, wq:])
    o_ref[...] = part.astype(BF16)
    x = x_ref[...].astype(F32)
    scale = lax.rsqrt(jnp.mean(x * x, axis=1, keepdims=True) + EPS)
    total = jnp.sum(part * (x * scale), axis=0, keepdims=True)

    @pl.when(pl.program_id(0) == 0)
    def _():
        g_ref[...] = jnp.zeros_like(g_ref)

    g_ref[0:1, :] += total


def finish_kernel(dims, here_ref, *refs):
    ctx, shard_rows, wq, wk, q_real, k_real, mix_cols, q_all, kv_all = dims
    pieces, (qkv_ref, mix_ref, gain_ref) = refs[:ctx], refs[ctx:]
    here = here_ref[0]
    total = 0.0
    for s in range(ctx):
        total = total + pieces[s][shard_rows:, :].astype(F32)
    gain_ref[...] = total
    for h in range(ctx):

        @pl.when(here == h)
        def _(h=h):
            for s in range(ctx):
                j = h ^ s
                piece = pieces[s][:shard_rows, :].astype(F32)
                qkv_ref[:, j * q_real : (j + 1) * q_real] = piece[:, :q_real]
                start = q_all + j * k_real
                qkv_ref[:, start : start + k_real] = piece[:, wq : wq + k_real]
                start = q_all + kv_all + j * k_real
                qkv_ref[:, start : start + k_real] = piece[:, wq + wk : wq + wk + k_real]
                start = wq + 2 * wk
                mix_ref[:, j * mix_cols : (j + 1) * mix_cols] = piece[:, start : start + mix_cols]


def row_block(rows, width):
    return pl.BlockSpec((rows, width), lambda i: (i, 0))


def whole_block(*shape):
    return pl.BlockSpec(shape, lambda i: (0,) * len(shape))


def local(hidden_in, norm_attn, w_qkv, w_mix, norm_moe, w_in, w_out, routes, gates, cotangent):
    groups = lax.axis_size("fsdp")
    ctx = lax.axis_size("ctx")
    here = lax.axis_index("ctx")
    shard = lax.axis_index("fsdp")
    rows = hidden_in.shape[1]
    width = hidden_in.shape[2]
    seq = rows * ctx
    group = HEADS // KVH
    kv_heads = KVH // ctx
    q_real, k_real = kv_heads * group * HD, kv_heads * HD
    wq, wk = pad_to(q_real, 128), pad_to(k_real, 128)
    proj_cols = wq + 2 * wk
    per_expert = w_in.shape[0]
    experts = per_expert * groups
    capacity = 5 * rows * TOP // (4 * experts)
    shard_rows = w_qkv.shape[0]

    def partner(array, s):
        return lax.ppermute(array, "ctx", [(i, i ^ s) for i in range(ctx)])

    half = HD // 2
    frequency = 10000.0 ** (-jnp.arange(half, dtype=F32) / half)
    angles = jnp.arange(seq, dtype=jnp.int32).astype(F32)[:, None] * frequency[None, :]
    cos_half, sin_half = jnp.cos(angles), jnp.sin(angles)
    cos_table = jnp.concatenate([cos_half] * 4, axis=1)
    sin_table = jnp.concatenate([-sin_half, sin_half] * 2, axis=1)

    def gather_ctx(array, placed):
        n = array.shape[0]
        total = placed(None, array, 0, here)
        if ctx == 4:
            near, far = partner(array, 1), partner(array, 2)
            total = placed(total, near, 0, here ^ 1)
            total = placed(total, far, 0, here ^ 2)
            total = placed(total, partner(near[: n // 2], 2), 0, here ^ 3)
            return placed(total, partner(far[n // 2 :], 1), n // 2, here ^ 3)
        for s in range(1, ctx):
            total = placed(total, partner(array, s), 0, here ^ s)
        return total

    own = hidden_in[0]

    def place_rows(total, piece, first, block):
        total = jnp.zeros((seq, width), BF16) if total is None else total
        return lax.dynamic_update_slice_in_dim(total, piece, block * rows + first, 0)

    x_all = gather_ctx(own, place_rows)

    def columns_of(matrix):
        return jnp.concatenate(
            [
                pad_cols(lax.dynamic_slice_in_dim(matrix, here * q_real, q_real, 1), wq),
                pad_cols(lax.dynamic_slice_in_dim(matrix, HEADS * HD + here * k_real, k_real, 1), wk),
                pad_cols(
                    lax.dynamic_slice_in_dim(matrix, (HEADS + KVH) * HD + here * k_real, k_real, 1), wk
                ),
            ],
            axis=1,
        )

    extra = 16
    gains = pad_cols(jnp.stack([norm_attn, norm_moe]), proj_cols)
    gains = jnp.pad(gains, ((0, extra - 2), (0, 0)))
    mix_cols = width // ctx
    mix_part = lax.dynamic_slice_in_dim(w_mix, here * mix_cols, mix_cols, 1)
    mix_part = jnp.pad(mix_part, ((0, extra), (0, 0)))
    gathered = lax.all_gather(
        jnp.concatenate(
            [jnp.concatenate([columns_of(w_qkv), gains], axis=0), mix_part], axis=1
        ),
        "fsdp",
        axis=0,
        tiled=False,
    )
    head_w = gathered[:, :shard_rows, :proj_cols].reshape(width, proj_cols)
    mix_part = gathered[:, :shard_rows, proj_cols:].reshape(width, mix_cols)
    gain_one = gathered[:, shard_rows, :shard_rows].reshape(1, width).astype(F32)
    gain_two = gathered[:, shard_rows + 1, :shard_rows].reshape(1, width).astype(F32)

    def place_columns(total, piece, first, block):
        total = jnp.zeros((width, width), BF16) if total is None else total
        return lax.dynamic_update_slice(total, piece, (first, block * mix_cols))

    full_mix = gather_ctx(mix_part, place_columns)
    cot_start, gathered = lax.optimization_barrier((cotangent[0], gathered))
    cotangents = lax.all_gather(cot_start, "fsdp", axis=0, tiled=False)

    ring = groups // 2
    turn_z, core = shard // 2, shard % 2
    expert_ids = jnp.arange(experts, dtype=jnp.int32)
    named = routes[0][None, :, :] == expert_ids[:, None, None]
    dense_gates = jnp.sum(jnp.where(named, gates[0][None, :, :], 0.0), axis=2)
    gate_rows = lax.all_to_all(dense_gates, "fsdp", split_axis=0, concat_axis=0, tiled=True)
    gate_rows = gate_rows.reshape(groups, per_expert, rows)
    sources = [(turn_z + (ring - k)) % ring for k in range(ring)]
    gate_rows = jnp.stack(
        [
            jnp.stack(
                [
                    lax.dynamic_index_in_dim(gate_rows, 2 * z + (core ^ j), 0, keepdims=False)
                    for j in range(2)
                ],
                axis=1,
            )
            for z in sources
        ]
    )
    named_here = gate_rows > 0
    order = jnp.arange(rows, dtype=jnp.int32)
    triangle = (order[:, None] <= order[None, :]).astype(BF16)
    counts = jnp.dot(
        named_here.astype(BF16).reshape(-1, rows), triangle, preferred_element_type=F32
    ).reshape(gate_rows.shape)
    slot_rows = jnp.where(named_here, counts.astype(jnp.int32) - 1, -1)
    slot_rows, gate_rows, x_all = lax.optimization_barrier((slot_rows, gate_rows, x_all))

    a_all, query, keys, values = pl.pallas_call(
        functools.partial(qkv_kernel, (wq, wk, wk)),
        grid=(ctx,),
        in_specs=[
            row_block(rows, width),
            whole_block(1, width),
            whole_block(width, proj_cols),
            row_block(rows, 128),
            row_block(rows, 128),
        ],
        out_specs=[
            row_block(rows, width),
            row_block(rows, wq),
            row_block(rows, wk),
            row_block(rows, wk),
        ],
        out_shape=[
            jax.ShapeDtypeStruct((seq, width), BF16),
            jax.ShapeDtypeStruct((seq, wq), BF16),
            jax.ShapeDtypeStruct((seq, wk), BF16),
            jax.ShapeDtypeStruct((seq, wk), BF16),
        ],
        name="qkv",
    )(x_all, gain_one, head_w, cos_table, sin_table)

    heads = kv_heads * group
    mixed_heads, log_total = pl.pallas_call(
        functools.partial(attend_kernel, ctx, rows, kv_heads, group),
        grid=(ctx,),
        in_specs=[row_block(rows, wq), whole_block(seq, wk), whole_block(seq, wk)],
        out_specs=[row_block(rows, q_real), pl.BlockSpec((1, 8, rows), lambda i: (i, 0, 0))],
        out_shape=[
            jax.ShapeDtypeStruct((seq, q_real), BF16),
            jax.ShapeDtypeStruct((ctx, 8, rows), F32),
        ],
        name="attend",
    )(query, keys, values)

    mixed = jnp.zeros((rows, HEADS * HD), BF16)
    for s in range(ctx):
        piece = lax.dynamic_slice_in_dim(mixed_heads, (here ^ s) * rows, rows, 0)
        piece = piece if s == 0 else partner(piece, s)
        mixed = lax.dynamic_update_slice_in_dim(mixed, piece, (here ^ s) * q_real, 1)

    inputs = own.astype(F32)
    scale_one = rms_scale(inputs)
    unit_one = inputs * scale_one
    middle = inputs + jnp.dot(mixed, full_mix, preferred_element_type=F32)
    scale_two = rms_scale(middle)
    unit_two = middle * scale_two
    normed_two = (unit_two * gain_two).astype(BF16)

    def across(array):
        return lax.ppermute(array, "fsdp", [(i, i ^ 1) for i in range(groups)])

    def onward(array):
        return lax.ppermute(array, "fsdp", [(i, (i + 2) % groups) for i in range(groups)])

    g_pairs = cotangents.reshape(ring, 2, rows, width)
    saved = None
    arrived = normed_two
    running = None
    for k in range(ring):
        pair = (arrived, across(arrived))
        following = onward(arrived) if k < ring - 1 else None
        if running is not None:
            pair, running = lax.optimization_barrier((pair, running))
        place = jnp.stack([sources[k], core]).astype(jnp.int32)
        saved, db_mine, db_other = experts_unit(
            place, slot_rows, gate_rows, pair, g_pairs, w_in, w_out, capacity, k, saved
        )
        if following is not None:
            following, db_mine, db_other = lax.optimization_barrier((following, db_mine, db_other))
        share = db_mine.astype(F32) + across(db_other).astype(F32)
        if k == 0:
            own_share = share
        else:
            if k > 1:
                share = share + onward(running).astype(F32)
            running = share.astype(BF16)
        arrived = following
    d_normed_two = own_share
    if ring > 1:
        d_normed_two = d_normed_two + onward(running).astype(F32)

    y_parts, gate_grad = saved[0], saved[1]
    y_sum = lax.psum_scatter(
        y_parts.reshape(groups, rows, width), "fsdp", scatter_dimension=0, tiled=False
    )
    gate_grad = gate_grad.transpose(0, 2, 1, 3).reshape(groups * per_expert, rows)
    gate_grad = lax.all_to_all(gate_grad, "fsdp", split_axis=0, concat_axis=0, tiled=True)
    gate_grad = jnp.sum(jnp.where(named, gate_grad[:, :, None], 0.0), axis=0)

    bits = ctx.bit_length() - 1
    expert_grads = []
    for e in range(per_expert):
        total = weight_grads(saved[2:], e, width // 2)
        total = total.reshape((2,) * bits + (width // ctx, total.shape[1]))
        left = list(range(bits))[::-1]
        for i in range(bits):
            bit = (i + e) % bits
            axis = left.index(bit)
            mine = (here >> bit) & 1
            kept = lax.dynamic_index_in_dim(total, mine, axis, keepdims=False)
            sent = lax.dynamic_index_in_dim(total, 1 - mine, axis, keepdims=False)
            total = kept.astype(F32) + partner(sent, 1 << bit).astype(F32)
            left.remove(bit)
            if i < bits - 1:
                total = total.astype(BF16)
        expert_grads.append(total)
    grad_in_part = jnp.stack([g[:, : 2 * F] for g in expert_grads])
    grad_out_part = jnp.stack([g[:, 2 * F :] for g in expert_grads])

    grad_out = cotangent[0].astype(F32)
    outputs = middle + y_sum.astype(F32)
    grad_gain_two = jnp.sum(d_normed_two * unit_two, axis=0)
    scaled_two = d_normed_two * gain_two
    d_middle = grad_out + scale_two * (
        scaled_two - unit_two * jnp.mean(scaled_two * unit_two, axis=-1, keepdims=True)
    )
    d_branch = d_middle.astype(BF16)
    d_mixed = lax.dot_general(
        d_branch, full_mix, (((1,), (1,)), ((), ())), preferred_element_type=F32
    ).astype(BF16)
    d_heads = jnp.zeros((ctx, rows, q_real), BF16)
    for s in range(ctx):
        piece = lax.dynamic_slice_in_dim(d_mixed, (here ^ s) * q_real, q_real, 1)
        piece = piece if s == 0 else partner(piece, s)
        d_heads = lax.dynamic_update_index_in_dim(d_heads, piece, here ^ s, 0)
    d_heads = d_heads.reshape(seq, q_real)

    grad_mix_local = lax.dot_general(
        mixed, d_branch, (((0,), (0,)), ((), ())), preferred_element_type=F32
    )

    d_query, d_keys_values = pl.pallas_call(
        functools.partial(attend_back_kernel, ctx, rows, kv_heads, group),
        grid=(ctx,),
        in_specs=[
            row_block(rows, wq),
            whole_block(seq, wk),
            whole_block(seq, wk),
            row_block(rows, q_real),
            pl.BlockSpec((1, 8, rows), lambda i: (i, 0, 0)),
            row_block(rows, 128),
            row_block(rows, 128),
            whole_block(seq, 128),
            whole_block(seq, 128),
        ],
        out_specs=[row_block(rows, wq), whole_block(seq, 2 * wk)],
        out_shape=[
            jax.ShapeDtypeStruct((seq, wq), BF16),
            jax.ShapeDtypeStruct((seq, 2 * wk), BF16),
        ],
        scratch_shapes=[
            pltpu.VMEM((seq, wk), F32),
            pltpu.VMEM((seq, wk), F32),
            pltpu.VMEM((rows, wq), F32),
        ],
        name="attend_back",
    )(query, keys, values, d_heads, log_total, cos_table, sin_table, cos_table, sin_table)
    d_normed_part, gain_one_part = pl.pallas_call(
        input_grad_kernel,
        grid=(ctx,),
        in_specs=[
            row_block(rows, wq),
            row_block(rows, 2 * wk),
            whole_block(width, proj_cols),
            row_block(rows, width),
        ],
        out_specs=[row_block(rows, width), whole_block(8, width)],
        out_shape=[
            jax.ShapeDtypeStruct((seq, width), BF16),
            jax.ShapeDtypeStruct((8, width), F32),
        ],
        name="input_grad",
    )(d_query, d_keys_values, head_w, x_all)
    d_normed_one = 0.0
    for s in range(ctx):
        piece = lax.dynamic_slice_in_dim(d_normed_part, (here ^ s) * rows, rows, 0)
        piece = piece if s == 0 else partner(piece, s)
        d_normed_one = d_normed_one + piece.astype(F32)
    grad_gain_one = gain_one_part[0]
    scaled_one = d_normed_one * gain_one
    d_inputs = d_middle + scale_one * (
        scaled_one - unit_one * jnp.mean(scaled_one * unit_one, axis=-1, keepdims=True)
    )

    d_projected = jnp.concatenate([d_query, d_keys_values], axis=1)
    grad_qkv_local = lax.dot_general(
        a_all, d_projected, (((0,), (0,)), ((), ())), preferred_element_type=F32
    ).astype(BF16)
    grad_mix_cols = 0.0
    for s in range(ctx):
        piece = lax.dynamic_slice_in_dim(grad_mix_local, (here ^ s) * mix_cols, mix_cols, 1)
        piece = piece if s == 0 else partner(piece.astype(BF16), s).astype(F32)
        grad_mix_cols = grad_mix_cols + piece
    mix_sum = lax.psum_scatter(
        grad_mix_cols.astype(BF16), "fsdp", scatter_dimension=0, tiled=True
    )
    gain_grads = jnp.stack([grad_gain_one, grad_gain_two], axis=0).astype(BF16)
    gain_grads = gain_grads.reshape(2, groups, shard_rows).transpose(1, 0, 2)
    gain_grads = jnp.pad(
        gain_grads, ((0, 0), (0, extra - 2), (0, proj_cols - shard_rows))
    )
    qkv_sum = lax.psum_scatter(
        jnp.concatenate([grad_qkv_local.reshape(groups, shard_rows, proj_cols), gain_grads], axis=1),
        "fsdp",
        scatter_dimension=0,
        tiled=False,
    )
    final = jnp.concatenate(
        [qkv_sum, jnp.pad(mix_sum, ((0, extra), (0, 0)))], axis=1
    )
    pieces = [final if s == 0 else partner(final, s) for s in range(ctx)]
    total_qkv, total_mix, gain_sums = pl.pallas_call(
        functools.partial(
            finish_kernel,
            (ctx, shard_rows, wq, wk, q_real, k_real, mix_cols, HEADS * HD, KVH * HD),
        ),
        in_specs=[pl.BlockSpec(memory_space=pltpu.SMEM)]
        + [pl.BlockSpec(memory_space=pltpu.VMEM)] * ctx,
        out_specs=[pl.BlockSpec(memory_space=pltpu.VMEM)] * 3,
        out_shape=[
            jax.ShapeDtypeStruct((shard_rows, (HEADS + 2 * KVH) * HD), F32),
            jax.ShapeDtypeStruct((shard_rows, width), F32),
            jax.ShapeDtypeStruct((extra, final.shape[1]), F32),
        ],
        name="finish",
    )(here.reshape(1), *pieces)
    total_one = gain_sums[0, :shard_rows]
    total_two = gain_sums[1, :shard_rows]
    return (
        outputs.astype(BF16)[None],
        d_inputs[None],
        total_one,
        total_qkv,
        total_mix,
        total_two,
        grad_in_part,
        grad_out_part,
        gate_grad[None],
    )


def solution(mesh):
    placed = (
        P("fsdp", "ctx", None),
        P("fsdp"),
        P("fsdp", None),
        P("fsdp", None),
        P("fsdp"),
        P("fsdp", None, None),
        P("fsdp", None, None),
        P("fsdp", "ctx", None),
        P("fsdp", "ctx", None),
        P("fsdp", "ctx", None),
    )
    return jax.shard_map(
        local,
        mesh=mesh,
        in_specs=placed,
        out_specs=(
            P("fsdp", "ctx", None),
            P("fsdp", "ctx", None),
            P("fsdp"),
            P("fsdp", None),
            P("fsdp", None),
            P("fsdp"),
            P("fsdp", "ctx", None),
            P("fsdp", "ctx", None),
            P("fsdp", "ctx", None),
        ),
        check_vma=False,
    )
```

```python
import functools

import jax
import jax.numpy as jnp
from jax import lax
from jax.experimental import pallas as pl
from jax.experimental.pallas import tpu as pltpu
from jax.sharding import PartitionSpec as P

HEADS = 24
KVH = 8
HD = 64
F = 512
TOP = 8
EPS = 1e-05
F32 = jnp.float32
BF16 = jnp.bfloat16


def rms_scale(values):
    return lax.rsqrt(jnp.mean(values * values, axis=-1, keepdims=True) + EPS)


def pad_to(width, unit):
    return -(-width // unit) * unit


def pad_cols(array, width):
    if array.shape[1] == width:
        return array
    return jnp.pad(array, ((0, 0), (0, width - array.shape[1])))


def swap_halves(values):
    lane = lax.broadcasted_iota(jnp.int32, values.shape, 1)
    return jnp.where(
        lane % HD < HD // 2,
        pltpu.roll(values, values.shape[1] - HD // 2, 1),
        pltpu.roll(values, HD // 2, 1),
    )


def turn(values, cosine, sine, sign):
    pieces = []
    for start in range(0, values.shape[1], 128):
        tile = values[:, start : start + 128]
        pieces.append(tile * cosine + sign * (swap_halves(tile) * sine))
    return pieces[0] if len(pieces) == 1 else jnp.concatenate(pieces, axis=1)


def qkv_kernel(widths, x_ref, gain_ref, w_ref, cos_ref, sin_ref, a_ref, q_ref, k_ref, v_ref):
    wq, wk, wv = widths
    x = x_ref[...].astype(F32)
    scale = lax.rsqrt(jnp.mean(x * x, axis=1, keepdims=True) + EPS)
    a = (x * scale * gain_ref[...]).astype(BF16)
    a_ref[...] = a
    proj = jnp.dot(a, w_ref[...], preferred_element_type=F32)
    cosine = cos_ref[...]
    sine = sin_ref[...]
    q_ref[...] = turn(proj[:, :wq], cosine, sine, 1.0).astype(BF16)
    k_ref[...] = turn(proj[:, wq : wq + wk], cosine, sine, 1.0).astype(BF16)
    v_ref[...] = proj[:, wq + wk :].astype(BF16)


def nt(left, right):
    return lax.dot_general(left, right, (((1,), (1,)), ((), ())), preferred_element_type=F32)


def tn(left, right):
    return lax.dot_general(left, right, (((0,), (0,)), ((), ())), preferred_element_type=F32)


def causal(keys, rows, start):
    key = lax.broadcasted_iota(jnp.int32, (keys, rows), 0)
    query = lax.broadcasted_iota(jnp.int32, (keys, rows), 1) + start
    return key <= query


def attend_kernel(blocks, rows, kv_heads, group, q_ref, k_ref, v_ref, o_ref, l_ref):
    step = pl.program_id(0)
    for block in range(blocks):

        @pl.when(step == block)
        def _(block=block):
            keys = (block + 1) * rows
            allowed = causal(keys, rows, block * rows)
            l_ref[...] = jnp.zeros_like(l_ref)
            for g in range(kv_heads):
                key = k_ref[:keys, g * HD : (g + 1) * HD]
                value = v_ref[:keys, g * HD : (g + 1) * HD]
                for r in range(group):
                    h = g * group + r
                    query = q_ref[:, h * HD : (h + 1) * HD]
                    scores = jnp.where(allowed, nt(key, query) * HD**-0.5, -1e30)
                    top = jnp.max(scores, axis=0, keepdims=True)
                    weights = jnp.exp(scores - top)
                    total = jnp.sum(weights, axis=0, keepdims=True)
                    out = tn(value, weights.astype(BF16)) / total
                    o_ref[:, h * HD : (h + 1) * HD] = out.T.astype(BF16)
                    l_ref[0, h : h + 1, :] = top + jnp.log(total)


def attend_back_kernel(
    blocks, rows, kv_heads, group, here_ref, q_ref, k_ref, v_ref, l_ref, cosq_ref, sinq_ref,
    cos_ref, sin_ref, *refs,
):
    pieces, (dq_ref, dkv_ref, dk_acc, dv_acc, dq_acc, d_ref) = refs[:blocks], refs[blocks:]
    step = pl.program_id(0)
    for s in range(blocks):

        @pl.when((here_ref[0] ^ s) == step)
        def _(s=s):
            d_ref[...] = pieces[s][...]

    @pl.when(step == 0)
    def _():
        dk_acc[...] = jnp.zeros_like(dk_acc)
        dv_acc[...] = jnp.zeros_like(dv_acc)
        dq_acc[...] = jnp.zeros_like(dq_acc)

    for block in range(blocks):

        @pl.when(step == block)
        def _(block=block):
            keys = (block + 1) * rows
            allowed = causal(keys, rows, block * rows)
            for g in range(kv_heads):
                lanes = slice(g * HD, (g + 1) * HD)
                key = k_ref[:keys, lanes]
                value = v_ref[:keys, lanes]
                dk = None
                dv = None
                for r in range(group):
                    h = g * group + r
                    query = q_ref[:, h * HD : (h + 1) * HD]
                    d_out = d_ref[:, h * HD : (h + 1) * HD]
                    scores = jnp.where(allowed, nt(key, query) * HD**-0.5, -1e30)
                    weights = jnp.exp(scores - l_ref[0, h : h + 1, :])
                    d_weights = nt(value, d_out)
                    delta = jnp.sum(weights * d_weights, axis=0, keepdims=True)
                    d_scores = (HD**-0.5 * weights * (d_weights - delta)).astype(BF16)
                    dq_acc[:, h * HD : (h + 1) * HD] = tn(key, d_scores).T
                    dk_part = jnp.dot(d_scores, query, preferred_element_type=F32)
                    dv_part = jnp.dot(weights.astype(BF16), d_out, preferred_element_type=F32)
                    dk = dk_part if dk is None else dk + dk_part
                    dv = dv_part if dv is None else dv + dv_part
                dk_acc[:keys, lanes] += dk
                dv_acc[:keys, lanes] += dv

    dq_ref[...] = turn(dq_acc[...], cosq_ref[...], sinq_ref[...], -1.0).astype(BF16)

    @pl.when(step == blocks - 1)
    def _():
        wk = dk_acc.shape[1]
        dkv_ref[:, :wk] = turn(dk_acc[...], cos_ref[...], sin_ref[...], -1.0).astype(BF16)
        dkv_ref[:, wk:] = dv_acc[...].astype(BF16)


def mm(left, right):
    return jnp.dot(left, right, preferred_element_type=F32)


def expert_kernel(dims, place_ref, slot_ref, gate_ref, b0_ref, b1_ref, g_ref, win_ref, wout_ref, *refs):
    rows, capacity, units, with_saved = dims
    refs = refs[5:] if with_saved else refs
    gg_ref, x_ref, r_ref, h_ref, p_ref, y0_ref, y1_ref, db0_ref, db1_ref, y_acc, db_acc = refs
    e = pl.program_id(0)
    core = place_ref[1]
    b_refs = (b0_ref, b1_ref)
    slots = lax.broadcasted_iota(jnp.int32, (capacity, rows), 0)
    picks, gate_cols = [], []
    for k in range(2):
        pick = slots == slot_ref[0, 0, k : k + 1, :]
        gate_cols.append(
            jnp.sum(jnp.where(pick, gate_ref[0, 0, k : k + 1, :], 0.0), axis=1, keepdims=True)
        )
        picks.append(pick.astype(F32).astype(BF16))
        x_ref[0, k * capacity : (k + 1) * capacity, :] = mm(picks[k], b_refs[k][...]).astype(BF16)
    win = win_ref[0]
    wout = wout_ref[0]
    paired = mm(x_ref[0], win)
    gate_part, up_part = paired[:, :units], paired[:, units:]
    sig = jax.nn.sigmoid(gate_part)
    silu = gate_part * sig
    hidden = (silu * up_part).astype(BF16)
    h_ref[0] = hidden
    result = nt(hidden, wout)
    gate_grads = []
    for k in range(2):
        part = slice(k * capacity, (k + 1) * capacity)
        cot = mm(picks[k], g_ref[0, core ^ k])
        r_ref[0, part, :] = (cot * gate_cols[k]).astype(BF16)
        gate_grad = jnp.sum(cot * result[part], axis=1, keepdims=True)
        gate_grads.append(jnp.sum(picks[k].astype(F32) * gate_grad, axis=0, keepdims=True))
        y_part = tn(picks[k], (result[part] * gate_cols[k]).astype(BF16))
        y_acc[k] = jnp.where(e == 0, y_part, y_acc[k] + y_part)
    gg_ref[0, 0] = jnp.where(
        core == 0,
        jnp.concatenate(gate_grads, axis=0),
        jnp.concatenate(gate_grads[::-1], axis=0),
    )
    d_hidden = mm(r_ref[0], wout)
    d_gate = d_hidden * up_part * sig * (1.0 + gate_part * (1.0 - sig))
    d_up = d_hidden * silu
    p_ref[0, :, :units] = d_gate.astype(BF16)
    p_ref[0, :, units:] = d_up.astype(BF16)
    d_rows = nt(p_ref[0], win).astype(BF16)
    for k in range(2):
        db_part = tn(picks[k], d_rows[k * capacity : (k + 1) * capacity])
        db_acc[k] = jnp.where(e == 0, db_part, db_acc[k] + db_part)

    @pl.when(e == pl.num_programs(0) - 1)
    def _():
        y0_ref[...] = y_acc[0].astype(BF16)
        y1_ref[...] = y_acc[1].astype(BF16)
        db0_ref[...] = db_acc[0].astype(BF16)
        db1_ref[...] = db_acc[1].astype(BF16)


def experts_unit(place, slot, gate, b_pair, g, w_in, w_out, capacity, unit, saved):
    per_expert, width, double = w_in.shape
    units = w_out.shape[2]
    ring, _, rows, _ = g.shape
    slots = 2 * capacity
    widths = (width, width, units, 2 * units)
    per_e = lambda *s: pl.BlockSpec((1,) + s, lambda e, p: (e,) + (0,) * len(s))
    whole = lambda *s: pl.BlockSpec(s, lambda e, p: (0,) * len(s))
    token_spec = pl.BlockSpec((1, 2, rows, width), lambda e, p: (p[0], 0, 0, 0))
    gate_spec = pl.BlockSpec((1, 1, 2, rows), lambda e, p: (unit, e, 0, 0))
    in_specs = [gate_spec, gate_spec, whole(rows, width), whole(rows, width), token_spec]
    in_specs += [per_e(width, double), per_e(width, units)]
    args = [place, slot, gate, *b_pair, g, w_in, w_out]
    aliases = {}
    if saved is not None:
        in_specs += [pl.BlockSpec(memory_space=pl.ANY)] * 5
        args += list(saved)
        aliases = {8 + i: i for i in range(5)}
    out = pl.pallas_call(
        functools.partial(expert_kernel, (rows, capacity, units, saved is not None)),
        grid_spec=pltpu.PrefetchScalarGridSpec(
            num_scalar_prefetch=1,
            grid=(per_expert,),
            in_specs=in_specs,
            out_specs=[
                pl.BlockSpec((1, 1, 2, rows), lambda e, p: (p[0], e, 0, 0)),
                *[pl.BlockSpec((1, slots, w), lambda e, p: (e, unit, 0)) for w in widths],
                *[whole(rows, width)] * 4,
            ],
            scratch_shapes=[pltpu.VMEM((2, rows, width), F32)] * 2,
        ),
        out_shape=[
            jax.ShapeDtypeStruct((ring, per_expert, 2, rows), F32),
            *[jax.ShapeDtypeStruct((per_expert, ring * slots, w), BF16) for w in widths],
            *[jax.ShapeDtypeStruct((rows, width), BF16)] * 4,
        ],
        input_output_aliases=aliases,
        compiler_params=pltpu.CompilerParams(vmem_limit_bytes=56 * 2**20),
        name="experts",
    )(*args)
    return out[:5], out[5:7], out[7:9]


def without_bit(p, bit):
    return (p & ((1 << bit) - 1)) | ((p >> (bit + 1)) << bit)


def store_halves(outs, p, value):
    half = value.shape[0] // 2
    for h in range(2):
        outs[2 * h + ((p >> h) & 1)][without_bit(p, h)] = value[h * half : (h + 1) * half]


def weight_kernel(dims, here_ref, x_ref, p_ref, r_ref, h_ref, *outs):
    per_tile, tiles = dims
    step = pl.program_id(0)
    grad_in = tn(x_ref[0], p_ref[0]).astype(BF16)
    grad_out = tn(r_ref[0], h_ref[0]).astype(BF16)
    total = jnp.concatenate([grad_in, grad_out], axis=1)
    rows = total.shape[0] // per_tile
    for v in range(per_tile):
        for i in range(tiles):

            @pl.when(jnp.logical_and(here_ref[0] % per_tile == v, step == i))
            def _(v=v, i=i):
                for j in range(per_tile):
                    store_halves(
                        outs, per_tile * i + (j ^ v), total[j * rows : (j + 1) * rows]
                    )


def weight_grads(here, saved, e, ctx):
    x, r, h, p = saved
    _, total, width = x.shape
    units = h.shape[2]
    rows = width // ctx
    per_tile = 1 if rows % 128 == 0 else 2
    tiles = ctx // per_tile
    tiled = pl.BlockSpec((1, total, per_tile * rows), lambda i, n: (e, 0, (n[0] // per_tile) ^ i))
    out = jax.ShapeDtypeStruct((ctx // 2, rows // 2, 3 * units), BF16)
    return pl.pallas_call(
        functools.partial(weight_kernel, (per_tile, tiles)),
        grid_spec=pltpu.PrefetchScalarGridSpec(
            num_scalar_prefetch=1,
            grid=(tiles,),
            in_specs=[
                tiled,
                pl.BlockSpec((1, total, 2 * units), lambda i, n: (e, 0, 0)),
                tiled,
                pl.BlockSpec((1, total, units), lambda i, n: (e, 0, 0)),
            ],
            out_specs=[pl.BlockSpec(out.shape, lambda i, n: (0, 0, 0))] * 4,
        ),
        out_shape=[out] * 4,
        compiler_params=pltpu.CompilerParams(vmem_limit_bytes=56 * 2**20),
        name="weight_grads",
    )(here, x, p, r, h)


def input_grad_kernel(ctx, here_ref, dq_ref, dkv_ref, w_ref, x_ref, g_ref, *outs):
    step = pl.program_id(0)
    wq = dq_ref.shape[1]
    part = nt(dq_ref[...], w_ref[:, :wq]) + nt(dkv_ref[...], w_ref[:, wq:])
    x = x_ref[...].astype(F32)
    scale = lax.rsqrt(jnp.mean(x * x, axis=1, keepdims=True) + EPS)
    total = jnp.sum(part * (x * scale), axis=0, keepdims=True)

    @pl.when(step == 0)
    def _():
        g_ref[...] = jnp.zeros_like(g_ref)

    g_ref[0:1, :] += total
    part = part.astype(BF16)
    for p in range(ctx):

        @pl.when(step == p)
        def _(p=p):
            store_halves(outs, p, part)


def mix_kernel(ctx, here_ref, x_ref, gain_ref, w_ref, *refs):
    pieces, (mid_ref, b_ref) = refs[:ctx], refs[ctx:]
    rows = pieces[0].shape[1]
    total = x_ref[...].astype(F32)
    for s in range(ctx):
        start = pl.multiple_of((here_ref[0] ^ s) * rows, rows)
        total = total + mm(pieces[s][...], w_ref[pl.ds(start, rows), :])
    mid_ref[...] = total
    scale = lax.rsqrt(jnp.mean(total * total, axis=1, keepdims=True) + EPS)
    b_ref[...] = (total * scale * gain_ref[...]).astype(BF16)


def middle_kernel(ctx, here_ref, own_ref, got_ref, mid_ref, cot_ref, gain_ref, w_ref, *refs):
    dmid_ref, branch_ref, g_ref = refs[:3]
    pieces = refs[3:]
    rows = pieces[0].shape[1]
    d_normed = own_ref[...].astype(F32) + got_ref[...].astype(F32)
    middle = mid_ref[...]
    scale = lax.rsqrt(jnp.mean(middle * middle, axis=1, keepdims=True) + EPS)
    unit = middle * scale
    g_ref[...] = jnp.broadcast_to(
        jnp.sum(d_normed * unit, axis=0, keepdims=True), g_ref.shape
    )
    scaled = d_normed * gain_ref[...]
    d_middle = cot_ref[...].astype(F32) + scale * (
        scaled - unit * jnp.mean(scaled * unit, axis=1, keepdims=True)
    )
    dmid_ref[...] = d_middle
    branch = d_middle.astype(BF16)
    branch_ref[...] = branch
    for s in range(ctx):
        start = pl.multiple_of((here_ref[0] ^ s) * rows, rows)
        pieces[s][...] = nt(branch, w_ref[pl.ds(start, rows), :]).astype(BF16)


def mix_grad_kernel(ctx, here_ref, d_ref, *refs):
    pieces, o_ref = refs[:ctx], refs[ctx]
    step = pl.program_id(0)
    for s in range(ctx):

        @pl.when(step == s)
        def _(s=s):
            o_ref[...] = tn(pieces[s][...], d_ref[...]).astype(BF16)


def finish_kernel(dims, here_ref, *refs):
    ctx, shard_rows, wq, wk, q_real, k_real, mix_cols, q_all, kv_all = dims
    pieces, (qkv_ref, mix_ref, gain_ref) = refs[:ctx], refs[ctx:]
    here = here_ref[0]
    total = 0.0
    for s in range(ctx):
        total = total + pieces[s][shard_rows:, :].astype(F32)
    gain_ref[...] = total
    for h in range(ctx):

        @pl.when(here == h)
        def _(h=h):
            for s in range(ctx):
                j = h ^ s
                piece = pieces[s][:shard_rows, :].astype(F32)
                qkv_ref[:, j * q_real : (j + 1) * q_real] = piece[:, :q_real]
                start = q_all + j * k_real
                qkv_ref[:, start : start + k_real] = piece[:, wq : wq + k_real]
                start = q_all + kv_all + j * k_real
                qkv_ref[:, start : start + k_real] = piece[:, wq + wk : wq + wk + k_real]
                start = wq + 2 * wk
                mix_ref[:, j * mix_cols : (j + 1) * mix_cols] = piece[:, start : start + mix_cols]


def row_block(rows, width):
    return pl.BlockSpec((rows, width), lambda i: (i, 0))


def whole_block(*shape):
    return pl.BlockSpec(shape, lambda i: (0,) * len(shape))


def local(hidden_in, norm_attn, w_qkv, w_mix, norm_moe, w_in, w_out, routes, gates, cotangent):
    groups = lax.axis_size("fsdp")
    ctx = lax.axis_size("ctx")
    here = lax.axis_index("ctx")
    shard = lax.axis_index("fsdp")
    rows = hidden_in.shape[1]
    width = hidden_in.shape[2]
    seq = rows * ctx
    group = HEADS // KVH
    kv_heads = KVH // ctx
    q_real, k_real = kv_heads * group * HD, kv_heads * HD
    wq, wk = pad_to(q_real, 128), pad_to(k_real, 128)
    proj_cols = wq + 2 * wk
    per_expert = w_in.shape[0]
    experts = per_expert * groups
    capacity = 5 * rows * TOP // (4 * experts)
    shard_rows = w_qkv.shape[0]

    bits = ctx.bit_length() - 1
    here_ref = here.reshape(1)
    vmem = pl.BlockSpec(memory_space=pltpu.VMEM)
    smem = pl.BlockSpec(memory_space=pltpu.SMEM)

    def partner(array, s):
        return lax.ppermute(array, "ctx", [(i, i ^ s) for i in range(ctx)])

    def tie(value, *others):
        return lax.optimization_barrier((value, *others))[0]

    def reduce_ctx(kept, sent, first):
        left = [bit for bit in range(bits) if bit != first]
        total = kept.astype(F32) + partner(sent, 1 << first).astype(F32)
        while left:
            total = total.astype(BF16)
            total = total.reshape((2, -1) + total.shape[1:])
            bit = left.pop()
            total = total[0].astype(F32) + partner(total[1], 1 << bit).astype(F32)
        return total.reshape(total.shape[1:])

    half = HD // 2
    frequency = 10000.0 ** (-jnp.arange(half, dtype=F32) / half)
    angles = jnp.arange(seq, dtype=jnp.int32).astype(F32)[:, None] * frequency[None, :]
    cos_half, sin_half = jnp.cos(angles), jnp.sin(angles)
    cos_table = jnp.concatenate([cos_half] * 4, axis=1)
    sin_table = jnp.concatenate([-sin_half, sin_half] * 2, axis=1)

    def gather_ctx(array, placed):
        n = array.shape[0]
        total = placed(None, array, 0, here)
        if ctx == 4:
            near, far = partner(array, 1), partner(array, 2)
            total = placed(total, near, 0, here ^ 1)
            total = placed(total, far, 0, here ^ 2)
            total = placed(total, partner(near[: n // 2], 2), 0, here ^ 3)
            return placed(total, partner(far[n // 2 :], 1), n // 2, here ^ 3)
        for s in range(1, ctx):
            total = placed(total, partner(array, s), 0, here ^ s)
        return total

    own = hidden_in[0]

    def place_rows(total, piece, first, block):
        total = jnp.zeros((seq, width), BF16) if total is None else total
        return lax.dynamic_update_slice_in_dim(total, piece, block * rows + first, 0)

    x_all = gather_ctx(own, place_rows)

    def columns_of(matrix):
        return jnp.concatenate(
            [
                pad_cols(lax.dynamic_slice_in_dim(matrix, here * q_real, q_real, 1), wq),
                pad_cols(lax.dynamic_slice_in_dim(matrix, HEADS * HD + here * k_real, k_real, 1), wk),
                pad_cols(
                    lax.dynamic_slice_in_dim(matrix, (HEADS + KVH) * HD + here * k_real, k_real, 1), wk
                ),
            ],
            axis=1,
        )

    extra = 16
    gains = pad_cols(jnp.stack([norm_attn, norm_moe]), proj_cols)
    gains = jnp.pad(gains, ((0, extra - 2), (0, 0)))
    mix_cols = width // ctx
    mix_part = lax.dynamic_slice_in_dim(w_mix, here * mix_cols, mix_cols, 1)
    mix_part = jnp.pad(mix_part, ((0, extra), (0, 0)))
    gathered = lax.all_gather(
        jnp.concatenate(
            [jnp.concatenate([columns_of(w_qkv), gains], axis=0), mix_part], axis=1
        ),
        "fsdp",
        axis=0,
        tiled=False,
    )
    gathered, x_all, cot_start = lax.optimization_barrier((gathered, x_all, cotangent[0]))
    cotangents = lax.all_gather(cot_start, "fsdp", axis=0, tiled=False)
    head_w = gathered[:, :shard_rows, :proj_cols].reshape(width, proj_cols)
    mix_part = gathered[:, :shard_rows, proj_cols:].reshape(width, mix_cols)
    gain_one = gathered[:, shard_rows, :shard_rows].reshape(1, width).astype(F32)
    gain_two = gathered[:, shard_rows + 1, :shard_rows].reshape(1, width).astype(F32)

    def place_columns(total, piece, first, block):
        total = jnp.zeros((width, width), BF16) if total is None else total
        return lax.dynamic_update_slice(total, piece, (first, block * mix_cols))

    full_mix = gather_ctx(mix_part, place_columns)

    ring = groups // 2
    turn_z, core = shard // 2, shard % 2
    expert_ids = jnp.arange(experts, dtype=jnp.int32)
    named = routes[0][None, :, :] == expert_ids[:, None, None]
    dense_gates = jnp.sum(jnp.where(named, gates[0][None, :, :], 0.0), axis=2)
    gate_rows = lax.all_to_all(dense_gates, "fsdp", split_axis=0, concat_axis=0, tiled=True)
    gate_rows = gate_rows.reshape(groups, per_expert, rows)
    sources = [(turn_z + (ring - k)) % ring for k in range(ring)]
    gate_rows = jnp.stack(
        [
            jnp.stack(
                [
                    lax.dynamic_index_in_dim(gate_rows, 2 * z + (core ^ j), 0, keepdims=False)
                    for j in range(2)
                ],
                axis=1,
            )
            for z in sources
        ]
    )
    named_here = gate_rows > 0
    order = jnp.arange(rows, dtype=jnp.int32)
    triangle = (order[:, None] <= order[None, :]).astype(BF16)
    counts = jnp.dot(
        named_here.astype(BF16).reshape(-1, rows), triangle, preferred_element_type=F32
    ).reshape(gate_rows.shape)
    slot_rows = jnp.where(named_here, counts.astype(jnp.int32) - 1, -1)
    slot_rows, gate_rows, x_all = lax.optimization_barrier((slot_rows, gate_rows, x_all))

    a_all, query, keys, values = pl.pallas_call(
        functools.partial(qkv_kernel, (wq, wk, wk)),
        grid=(ctx,),
        in_specs=[
            row_block(rows, width),
            whole_block(1, width),
            whole_block(width, proj_cols),
            row_block(rows, 128),
            row_block(rows, 128),
        ],
        out_specs=[
            row_block(rows, width),
            row_block(rows, wq),
            row_block(rows, wk),
            row_block(rows, wk),
        ],
        out_shape=[
            jax.ShapeDtypeStruct((seq, width), BF16),
            jax.ShapeDtypeStruct((seq, wq), BF16),
            jax.ShapeDtypeStruct((seq, wk), BF16),
            jax.ShapeDtypeStruct((seq, wk), BF16),
        ],
        name="qkv",
    )(x_all, gain_one, head_w, cos_table, sin_table)

    heads = kv_heads * group
    mixed_heads, log_total = pl.pallas_call(
        functools.partial(attend_kernel, ctx, rows, kv_heads, group),
        grid=(ctx,),
        in_specs=[row_block(rows, wq), whole_block(seq, wk), whole_block(seq, wk)],
        out_specs=[row_block(rows, q_real), pl.BlockSpec((1, 8, rows), lambda i: (i, 0, 0))],
        out_shape=[
            jax.ShapeDtypeStruct((seq, q_real), BF16),
            jax.ShapeDtypeStruct((ctx, 8, rows), F32),
        ],
        name="attend",
    )(query, keys, values)

    mixed = []
    for s in range(ctx):
        piece = lax.dynamic_slice_in_dim(mixed_heads, (here ^ s) * rows, rows, 0)
        mixed.append(piece if s == 0 else partner(piece, s))
    middle, normed_two = pl.pallas_call(
        functools.partial(mix_kernel, ctx),
        in_specs=[smem] + [vmem] * (3 + ctx),
        out_specs=[vmem] * 2,
        out_shape=[
            jax.ShapeDtypeStruct((rows, width), F32),
            jax.ShapeDtypeStruct((rows, width), BF16),
        ],
        name="mix",
    )(here_ref, own, gain_two, full_mix, *mixed)

    def across(array):
        return lax.ppermute(array, "fsdp", [(i, i ^ 1) for i in range(groups)])

    def onward(array):
        return lax.ppermute(array, "fsdp", [(i, (i + 2) % groups) for i in range(groups)])

    g_pairs = cotangents.reshape(ring, 2, rows, width)
    saved = None
    arrived = normed_two
    running = None
    y_shares = []
    for k in range(ring):
        pair = (arrived, across(arrived))
        following = onward(arrived) if k < ring - 1 else None
        if running is not None:
            pair, running = lax.optimization_barrier((pair, running))
        place = jnp.stack([sources[k], core]).astype(jnp.int32)
        saved, (y_mine, y_other), (db_mine, db_other) = experts_unit(
            place, slot_rows, gate_rows, pair, g_pairs, w_in, w_out, capacity, k, saved
        )
        if following is not None:
            following, db_mine, db_other = lax.optimization_barrier((following, db_mine, db_other))
        share = db_mine.astype(F32) + across(db_other).astype(F32)
        if k == 0:
            own_share = share
        else:
            if k > 1:
                share = share + onward(running).astype(F32)
            running = share.astype(BF16)
        y_shares.append((y_mine, y_other))
        arrived = following
    last_share = onward(running)

    gate_grad = saved[0]
    gate_grad = gate_grad.transpose(0, 2, 1, 3).reshape(groups * per_expert, rows)
    gate_grad = lax.all_to_all(gate_grad, "fsdp", split_axis=0, concat_axis=0, tiled=True)
    gate_grad = jnp.sum(jnp.where(named, gate_grad[:, :, None], 0.0), axis=0)

    d_middle, d_branch, gain_two_part, *d_mixed = pl.pallas_call(
        functools.partial(middle_kernel, ctx),
        in_specs=[smem] + [vmem] * 6,
        out_specs=[vmem] * (3 + ctx),
        out_shape=[
            jax.ShapeDtypeStruct((rows, width), F32),
            jax.ShapeDtypeStruct((rows, width), BF16),
            jax.ShapeDtypeStruct((8, width), F32),
            *[jax.ShapeDtypeStruct((rows, q_real), BF16)] * ctx,
        ],
        name="middle",
    )(here_ref, own_share, last_share, middle, cotangent[0], gain_two, full_mix)
    grad_gain_two = gain_two_part[0]
    d_heads = [piece if s == 0 else partner(piece, s) for s, piece in enumerate(d_mixed)]

    y_running = None
    for k in list(range(1, ring)) + [0]:
        y_mine, y_other = y_shares[k]
        total = y_mine.astype(F32) + across(y_other).astype(F32)
        if y_running is not None:
            total = total + onward(y_running).astype(F32)
        if k != 0:
            y_running = total.astype(BF16)
            if k == 1:
                y_running = tie(y_running, last_share)
    outputs = middle + total

    expert_grads = []
    for e in range(per_expert):
        kept0, sent0, kept1, sent1 = weight_grads(here_ref, saved[1:], e, ctx)
        if e > 0:
            sent0, sent1 = lax.optimization_barrier((sent0, sent1, *d_heads))[:2]
        expert_grads.append(
            jnp.concatenate(
                [reduce_ctx(kept0, sent0, 0), reduce_ctx(kept1, sent1, min(1, bits - 1))], axis=0
            )
        )
    grad_in_part = jnp.stack([g[:, : 2 * F] for g in expert_grads])
    grad_out_part = jnp.stack([g[:, 2 * F :] for g in expert_grads])

    grad_mix_local = pl.pallas_call(
        functools.partial(mix_grad_kernel, ctx),
        grid_spec=pltpu.PrefetchScalarGridSpec(
            num_scalar_prefetch=1,
            grid=(ctx,),
            in_specs=[pl.BlockSpec((rows, width), lambda i, n: (0, 0))]
            + [pl.BlockSpec((rows, q_real), lambda i, n: (0, 0))] * ctx,
            out_specs=pl.BlockSpec((q_real, width), lambda i, n: (n[0] ^ i, 0)),
        ),
        out_shape=jax.ShapeDtypeStruct((HEADS * HD, width), BF16),
        name="mix_grad",
    )(here_ref, d_branch, *mixed)
    mix_rows = lax.psum_scatter(grad_mix_local, "fsdp", scatter_dimension=0, tiled=True)

    d_query, d_keys_values = pl.pallas_call(
        functools.partial(attend_back_kernel, ctx, rows, kv_heads, group),
        grid=(ctx,),
        in_specs=[
            smem,
            row_block(rows, wq),
            whole_block(seq, wk),
            whole_block(seq, wk),
            pl.BlockSpec((1, 8, rows), lambda i: (i, 0, 0)),
            row_block(rows, 128),
            row_block(rows, 128),
            whole_block(seq, 128),
            whole_block(seq, 128),
            *[whole_block(rows, q_real)] * ctx,
        ],
        out_specs=[row_block(rows, wq), whole_block(seq, 2 * wk)],
        out_shape=[
            jax.ShapeDtypeStruct((seq, wq), BF16),
            jax.ShapeDtypeStruct((seq, 2 * wk), BF16),
        ],
        scratch_shapes=[
            pltpu.VMEM((seq, wk), F32),
            pltpu.VMEM((seq, wk), F32),
            pltpu.VMEM((rows, wq), F32),
            pltpu.VMEM((rows, q_real), BF16),
        ],
        name="attend_back",
    )(
        here_ref, query, keys, values, log_total, cos_table, sin_table, cos_table, sin_table,
        *d_heads,
    )
    half_out = jax.ShapeDtypeStruct((ctx // 2, rows // 2, width), BF16)
    gain_one_part, kept0, sent0, kept1, sent1 = pl.pallas_call(
        functools.partial(input_grad_kernel, ctx),
        grid_spec=pltpu.PrefetchScalarGridSpec(
            num_scalar_prefetch=1,
            grid=(ctx,),
            in_specs=[
                pl.BlockSpec((rows, wq), lambda i, n: (n[0] ^ i, 0)),
                pl.BlockSpec((rows, 2 * wk), lambda i, n: (n[0] ^ i, 0)),
                pl.BlockSpec((width, proj_cols), lambda i, n: (0, 0)),
                pl.BlockSpec((rows, width), lambda i, n: (n[0] ^ i, 0)),
            ],
            out_specs=[pl.BlockSpec((8, width), lambda i, n: (0, 0))]
            + [pl.BlockSpec(half_out.shape, lambda i, n: (0, 0, 0))] * 4,
        ),
        out_shape=[jax.ShapeDtypeStruct((8, width), F32)] + [half_out] * 4,
        name="input_grad",
    )(here_ref, d_query, d_keys_values, head_w, x_all)
    d_normed_one = jnp.concatenate(
        [reduce_ctx(kept0, sent0, 0), reduce_ctx(kept1, sent1, min(1, bits - 1))], axis=0
    )
    grad_gain_one = gain_one_part[0]
    inputs = own.astype(F32)
    scale_one = rms_scale(inputs)
    unit_one = inputs * scale_one
    scaled_one = d_normed_one * gain_one
    d_inputs = d_middle + scale_one * (
        scaled_one - unit_one * jnp.mean(scaled_one * unit_one, axis=-1, keepdims=True)
    )

    d_projected = jnp.concatenate([d_query, d_keys_values], axis=1)
    grad_qkv_local = lax.dot_general(
        a_all, d_projected, (((0,), (0,)), ((), ())), preferred_element_type=F32
    ).astype(BF16)
    mix_sum = 0.0
    for s in range(ctx):
        piece = lax.dynamic_slice_in_dim(mix_rows, (here ^ s) * mix_cols, mix_cols, 1)
        mix_sum = mix_sum + (piece if s == 0 else partner(piece, s)).astype(F32)
    mix_sum = mix_sum.astype(BF16)
    gain_grads = jnp.stack([grad_gain_one, grad_gain_two], axis=0).astype(BF16)
    gain_grads = gain_grads.reshape(2, groups, shard_rows).transpose(1, 0, 2)
    gain_grads = jnp.pad(
        gain_grads, ((0, 0), (0, extra - 2), (0, proj_cols - shard_rows))
    )
    qkv_sum = lax.psum_scatter(
        jnp.concatenate([grad_qkv_local.reshape(groups, shard_rows, proj_cols), gain_grads], axis=1),
        "fsdp",
        scatter_dimension=0,
        tiled=False,
    )
    final = jnp.concatenate(
        [qkv_sum, jnp.pad(mix_sum, ((0, extra), (0, 0)))], axis=1
    )
    pieces = [final if s == 0 else partner(final, s) for s in range(ctx)]
    total_qkv, total_mix, gain_sums = pl.pallas_call(
        functools.partial(
            finish_kernel,
            (ctx, shard_rows, wq, wk, q_real, k_real, mix_cols, HEADS * HD, KVH * HD),
        ),
        in_specs=[pl.BlockSpec(memory_space=pltpu.SMEM)]
        + [pl.BlockSpec(memory_space=pltpu.VMEM)] * ctx,
        out_specs=[pl.BlockSpec(memory_space=pltpu.VMEM)] * 3,
        out_shape=[
            jax.ShapeDtypeStruct((shard_rows, (HEADS + 2 * KVH) * HD), F32),
            jax.ShapeDtypeStruct((shard_rows, width), F32),
            jax.ShapeDtypeStruct((extra, final.shape[1]), F32),
        ],
        name="finish",
    )(here.reshape(1), *pieces)
    total_one = gain_sums[0, :shard_rows]
    total_two = gain_sums[1, :shard_rows]
    return (
        outputs.astype(BF16)[None],
        d_inputs[None],
        total_one,
        total_qkv,
        total_mix,
        total_two,
        grad_in_part,
        grad_out_part,
        gate_grad[None],
    )


def solution(mesh):
    placed = (
        P("fsdp", "ctx", None),
        P("fsdp"),
        P("fsdp", None),
        P("fsdp", None),
        P("fsdp"),
        P("fsdp", None, None),
        P("fsdp", None, None),
        P("fsdp", "ctx", None),
        P("fsdp", "ctx", None),
        P("fsdp", "ctx", None),
    )
    return jax.shard_map(
        local,
        mesh=mesh,
        in_specs=placed,
        out_specs=(
            P("fsdp", "ctx", None),
            P("fsdp", "ctx", None),
            P("fsdp"),
            P("fsdp", None),
            P("fsdp", None),
            P("fsdp"),
            P("fsdp", "ctx", None),
            P("fsdp", "ctx", None),
            P("fsdp", "ctx", None),
        ),
        check_vma=False,
    )
```
